512 devices in a mesh: comp: 8 (over y), pts: 64 (over x, z, core).
Axes of the slice: x: 4, y: 8, z: 8, core: 2. Of those that a mesh axis runs over, the one named last changes fastest.
Arguments:
- spectrum: float32 [1296, 65536], P('comp', 'pts'), may hold values from 0.05 to 2
- courant: float32 [1296], P('comp'), may hold values from -0.9 to 0.9
- growth: float32 [1296], replicated, may hold values from 0 to 0.4
- quad_a: bfloat16 [640, 1296], replicated, may hold values from -0.15625 to 0.15625
- quad_b: bfloat16 [640, 1296], replicated, may hold values from -0.15625 to 0.15625
- sea_mask: int32 [65536], P('pts'), may hold values 0 or 1
- nest_counts: int32 [64], replicated, may hold values from 1 to 192, 6144 in all
- nest_offsets: int32 [6144], replicated, may hold values from 0 to 1023
Outputs:
- final_spectrum: float32 [1296, 65536], P('comp', 'pts')
- nest_boundary: float32 [1296, 6144], P('comp', 'pts')
The draws below stay inside these ranges and needn't reach their ends.
Inputs may be any that keep to these rules, and one draw needn't show every extreme that they name: nest_counts sum to 6144; the entries of block o are the consecutive entries after those of blocks before it; some block supplies exactly 192.
All inputs are finite; a program needn't handle non-finite values. No bound on the sum of `sea_mask` on one device may be relied on, other than what follows from the above.
Results may differ from the reference program's by a relative error of at most 0.0028.
Values sent between devices are 32-bit elements; how exact they have to be, the bound alone decides.
No kernel may reach another device: no remote copies, remote signals or barrier semaphores. Data moves between devices by JAX's collectives and lax.ppermute only.
A program may use at most 64 MiB of HBM per device.

```python
import math
import jax
import jax.numpy as jnp
import numpy as np
from jax import lax

K = 1296
Q = 640
PTS_DEV = 1024
NB = 6144
STEPS = 2
NP = 65536
NB_BLOCK = 192
N_PTS = 64


def with_ends(result, key, low, top_value):
    shape = result.shape
    place = [jax.random.randint(jax.random.fold_in(key, axis), (), 0, shape[axis]) for axis in range(len(shape))]
    result = result.at[tuple(place)].set(low)
    longest = shape.index(max(shape))
    place[longest] = (place[longest] + 1) % shape[longest]
    return result.at[tuple(place)].set(top_value)


def block_scale(key, dims, shards, low, largest):
    gain = 1.0
    for axis_at, blocks in shards:
        steps = jax.random.uniform(jax.random.fold_in(jax.random.fold_in(key, 6), axis_at), (blocks,), jnp.float32, low / len(shards), largest / len(shards))
        gain = gain * jnp.repeat(jnp.exp(steps), dims[axis_at] // blocks).reshape((-1,) + (1,) * (len(dims) - 1 - axis_at))
    return gain


def split_up(amount, total, reach, slope):
    loads = [(1 << 20) // math.isqrt(grade ** slope) + 1 for grade in range(2, amount + 1)]
    surplus, counts = total - reach - (amount - 1), [1] * (amount - 1)
    while surplus > 0:
        candidates = [i for i in range(amount - 1) if counts[i] < reach]
        mass, budget = sum([loads[i] for i in candidates]), surplus
        for i in candidates:
            extra = min(reach - counts[i], max(1, budget * loads[i] // mass), surplus)
            counts[i] = counts[i] + extra
            surplus = surplus - extra
    return np.array([reach] + counts)


def ragged(own_key, count, total, limit, skew):
    if count == 2:
        one = jax.random.randint(own_key, (), max(1, total - limit), min(limit, total - 1) + 1)
        return jnp.stack([one, total - one])
    sizes = jnp.asarray(split_up(count, total, limit, skew), jnp.int32)
    pairs = (count - 1) // 2
    donor, sink = sizes[1:1 + 2 * pairs:2], sizes[2:2 + 2 * pairs:2]
    slack = jnp.minimum(donor - 1, limit - sink)
    shifted = jax.random.randint(jax.random.fold_in(own_key, 1), (pairs,), 0, 1 << 20) % (slack + 1)
    sizes = sizes.at[1:1 + 2 * pairs:2].set(donor - shifted).at[2:2 + 2 * pairs:2].set(sink + shifted)
    return sizes[jax.random.permutation(jax.random.fold_in(own_key, 2), count)]


def normal_values(stream_key, dims, scale, bound, kind=jnp.bfloat16):
    drawn = scale * jax.random.normal(stream_key, dims, jnp.float32)
    return jnp.clip(drawn, min=-bound, max=bound).astype(kind)


def setup_inputs(seed: int = 0) -> dict:
    keys = jax.random.split(jax.random.key(seed), 9)
    return {
        "spectrum": jnp.clip(jnp.exp(math.log(2.0) - 3.6888794 * jax.random.uniform(keys[0], (K, NP), jnp.float32) ** block_scale(keys[0], (K, NP), ((0, 8), (1, 64)), -0.2, 0.2)), 0.05, 2.0),
        "courant": jnp.clip(jax.random.uniform(keys[1], (K,), jnp.float32, -0.9, 0.9) * block_scale(keys[1], (K,), ((0, 8),), -0.4, 0.0), -0.9, 0.9),
        "growth": jnp.clip(jax.random.uniform(keys[2], (K,), jnp.float32, 0.0, 0.4), 0.0, 0.4),
        "quad_a": normal_values(keys[3], (Q, K), K ** -0.5, 0.15625),
        "quad_b": normal_values(keys[4], (Q, K), K ** -0.5, 0.15625),
        "sea_mask": with_ends((jax.random.randint(keys[5], (NP,), 0, 5) < 4).astype(jnp.int32), jax.random.fold_in(keys[5], 1), 0, 1),
        "nest_counts": ragged(keys[6], N_PTS, NB, NB_BLOCK, 2).astype(jnp.int32),
        "nest_offsets": with_ends(jax.random.randint(keys[7], (NB,), 0, PTS_DEV), jax.random.fold_in(keys[7], 1), 0, PTS_DEV - 1).astype(jnp.int32),
    }


dissipation = 0.5

def propagate(field, courant, sea):
    padded = jnp.pad(field, ((0, 0), (1, 1)))
    upwind = jnp.where(courant[:, None] > 0, padded[:, :-2], padded[:, 2:])
    speed = jnp.abs(courant)[:, None]
    return ((1.0 - speed) * field + speed * upwind) * sea[None, :]

def source(moved, quad_a, quad_b, growth):
    rounded = moved.astype(jnp.bfloat16)
    left = jnp.dot(quad_a, rounded, preferred_element_type=jnp.float32)
    right = jnp.dot(quad_b, rounded, preferred_element_type=jnp.float32)
    pairs = (left * right).astype(jnp.bfloat16)
    transfer = lax.dot_general(quad_a, pairs, (((0,), (0,)), ((), ())), preferred_element_type=jnp.float32)
    spread = jnp.sqrt(lax.optimization_barrier(jnp.mean(moved * moved, axis=0)) + 1e-06)
    return (moved + growth[:, None] * moved + transfer) / (1.0 + dissipation * spread)[None, :]

def reference(spectrum, courant, growth, quad_a, quad_b, sea_mask, nest_counts, nest_offsets):
    sea = sea_mask.astype(jnp.float32)
    field = spectrum
    for step in range(STEPS):
        field = source(propagate(field, courant, sea), quad_a, quad_b, growth)
    ends = jnp.cumsum(nest_counts).astype(jnp.int32)
    index_b = jnp.arange(NB, dtype=jnp.int32)
    first = ((index_b + ends[0]) % NB).astype(jnp.int32)
    second = (index_b - NB // 2).astype(jnp.int32)
    entries = jnp.where(index_b < NB // 2, first, second).astype(jnp.int32)
    owner = lax.optimization_barrier(jnp.sum((ends[None, :] <= entries[:, None]).astype(jnp.int32), axis=1)).astype(jnp.int32)
    points = (owner * PTS_DEV + jnp.take(nest_offsets, entries)).astype(jnp.int32)
    nest = jnp.take(field, points, axis=1)
    return (field, nest)
```

```python
import functools

import jax
import jax.numpy as jnp
from jax import lax
from jax.experimental import pallas as pl
from jax.experimental.pallas import tpu as pltpu
from jax.sharding import PartitionSpec as P

STEPS = 2
LANES = 128
NB_BLOCK = 192
DISSIPATION = 0.5

F32 = jnp.float32
BF16 = jnp.bfloat16
VMEM = pl.BlockSpec(memory_space=pltpu.VMEM)
SMEM = pl.BlockSpec(memory_space=pltpu.SMEM)


def call(body, out_shape, n_in, smem=(), cost=None, scratch=()):
    specs = [SMEM if i in smem else VMEM for i in range(n_in)]
    outs = VMEM if not isinstance(out_shape, (tuple, list)) else tuple(VMEM for _ in out_shape)
    flops, bytes_accessed = cost or (1_000_000, 1_000_000)
    return pl.pallas_call(
        body,
        out_shape=out_shape,
        in_specs=specs,
        out_specs=outs,
        scratch_shapes=list(scratch),
        cost_estimate=pl.CostEstimate(flops=flops, bytes_accessed=bytes_accessed, transcendentals=0),
    )


def iota(shape, axis):
    return lax.broadcasted_iota(jnp.int32, shape, axis)


def split3(value):
    high = value.astype(BF16)
    rest = value - high.astype(F32)
    middle = rest.astype(BF16)
    low = (rest - middle.astype(F32)).astype(BF16)
    return high, middle, low


def exact_dot(value, chosen, dims):
    high, middle, low = (lax.dot_general(term, chosen, (dims, ((), ())), preferred_element_type=F32) for term in split3(value))
    return (high + middle) + low


def exact_pick(chosen, value):
    high, middle, low = (lax.dot_general(chosen, term, (((1,), (0,)), ((), ())), preferred_element_type=F32) for term in split3(value))
    return (high + middle) + low


def edges_body(field_ref, sea_ref, up_ref, down_ref):
    comps, points = field_ref.shape
    padded = up_ref.shape[1]
    for ref, start, order in ((up_ref, points - LANES, (LANES - 1, LANES - 2)), (down_ref, 0, (0, 1))):
        tile = field_ref[:, start:start + LANES]
        tile = jnp.concatenate([tile, jnp.zeros((padded - comps, LANES), F32)], axis=0)
        turned = tile.T
        for row, lane in enumerate(order):
            ref[row:row + 1, :] = turned[lane:lane + 1, :]
        sea = sea_ref[0:1, start + order[0]:start + order[0] + 1].astype(F32)
        ref[2:3, :] = jnp.broadcast_to(sea, (1, padded))
        ref[3:8, :] = jnp.zeros((5, padded), F32)


def pack_body(field_ref, sea_ref, courant_ref, before_ref, after_ref, out_ref):
    comps, points = field_ref.shape
    chunks = points // LANES
    padded = before_ref.shape[1]
    rows = jnp.concatenate(
        [before_ref[0:3, :], after_ref[0:3, :], jnp.concatenate([courant_ref[...], jnp.zeros((1, padded - comps), F32)], axis=1), jnp.zeros((1, padded), F32)],
        axis=0,
    )
    columns = rows.T[:comps, :]

    def wide(at):
        return jnp.broadcast_to(columns[:, at:at + 1], (comps, LANES))

    near_before, far_before, sea_before = wide(0), wide(1), wide(2)
    near_after, far_after, sea_after = wide(3), wide(4), wide(5)
    courant = wide(6)
    speed = jnp.abs(courant)
    stay = 1.0 - speed
    forward = courant > 0
    lane = iota((comps, LANES), 1)

    tiles = [field_ref[:, k * LANES:(k + 1) * LANES] for k in range(chunks)]
    moved = []
    for k in range(chunks):
        left_edge = near_before if k == 0 else jnp.broadcast_to(tiles[k - 1][:, LANES - 1:LANES], (comps, LANES))
        right_edge = near_after if k == chunks - 1 else jnp.broadcast_to(tiles[k + 1][:, 0:1], (comps, LANES))
        left = jnp.where(lane == 0, left_edge, pltpu.roll(tiles[k], 1, 1))
        right = jnp.where(lane == LANES - 1, right_edge, pltpu.roll(tiles[k], LANES - 1, 1))
        sea = sea_ref[0:1, k * LANES:(k + 1) * LANES].astype(F32)
        value = (stay * tiles[k] + speed * jnp.where(forward, left, right)) * sea
        out_ref[k, 0:comps, :] = value
        moved.append(value)

    first = jnp.broadcast_to(tiles[0][:, 0:1], (comps, LANES))
    last = jnp.broadcast_to(tiles[chunks - 1][:, LANES - 1:LANES], (comps, LANES))
    moved_before = (stay * near_before + speed * jnp.where(forward, far_before, first)) * sea_before
    moved_after = (stay * near_after + speed * jnp.where(forward, last, far_after)) * sea_after
    ghosts = courant
    for k in range(chunks):
        low = moved_before if k == 0 else jnp.broadcast_to(moved[k - 1][:, LANES - 1:LANES], (comps, LANES))
        high = moved_after if k == chunks - 1 else jnp.broadcast_to(moved[k + 1][:, 0:1], (comps, LANES))
        ghosts = jnp.where(lane == k, low, jnp.where(lane == chunks + k, high, ghosts))
    turned = jnp.concatenate([ghosts, jnp.zeros((padded - comps, LANES), F32)], axis=0).T
    for k in range(chunks):
        for at, source in ((0, k), (2, chunks + k), (4, 2 * chunks)):
            out_ref[k, comps + at:comps + at + 1, :] = turned[source:source + 1, 0:LANES]
            out_ref[k, comps + at + 1:comps + at + 2, :] = turned[source:source + 1, LANES:2 * LANES]


def steps_body(where_ref, slab_ref, a_ref, b_ref, turned_a_ref, growth_ref, sea_ref, out_ref, moved_ref, courant_ref, gain_ref, result_ref):
    groups, _, _ = slab_ref.shape
    comps = out_ref.shape[1]
    total = moved_ref.shape[0]
    lane = iota((comps, LANES), 1)
    for g in range(groups):
        start = g * comps
        moved_ref[start:start + comps, 0:LANES] = slab_ref[g, 0:comps, :]
        extra = slab_ref[g, comps:comps + 6, :]
        rows = jnp.concatenate([extra, jnp.zeros((2, LANES), F32)], axis=0)
        columns = rows.T
        tall = [jnp.concatenate([columns[:, 2 * i:2 * i + 1], columns[:comps - LANES, 2 * i + 1:2 * i + 2]], axis=0) for i in range(3)]
        low, high, courant = (jnp.broadcast_to(t, (comps, LANES)) for t in tall)
        moved_ref[start:start + comps, LANES:2 * LANES] = jnp.where(lane == 0, high, jnp.where(lane == LANES - 1, low, 0.0))
        courant_ref[start:start + comps, :] = courant
    growth = growth_ref[...]
    width = growth.shape[1]
    gain_ref[...] = jnp.broadcast_to(jnp.broadcast_to(growth, (8, width)).T[:, 0:1], (total, LANES))

    def source(moved, gain):
        rounded = moved.astype(BF16)
        left = jnp.dot(a_ref[...], rounded, preferred_element_type=F32)
        right = jnp.dot(b_ref[...], rounded, preferred_element_type=F32)
        pairs = (left * right).astype(BF16)
        transfer = jnp.dot(turned_a_ref[...], pairs, preferred_element_type=F32)
        mean = jnp.sum(moved * moved, axis=0, keepdims=True) / total
        spread = jnp.sqrt(mean + 1e-06)
        scale = 1.0 / (1.0 + DISSIPATION * spread)
        return (moved + gain * moved + transfer) * scale

    gain = gain_ref[...]
    moved = moved_ref[...]
    field = source(moved, jnp.concatenate([gain, gain], axis=1))
    left = pltpu.roll(field, 1, 1)[:, 0:LANES]
    right = pltpu.roll(field, 2 * LANES - 1, 1)[:, 0:LANES]
    courant = courant_ref[...]
    speed = jnp.abs(courant)
    sea = sea_ref[pl.ds(where_ref[0], 1), :].astype(F32)
    moved = ((1.0 - speed) * field[:, 0:LANES] + speed * jnp.where(courant > 0, left, right)) * sea
    result_ref[...] = source(moved, gain)
    for g in range(groups):
        out_ref[g, :, :] = result_ref[g * comps:(g + 1) * comps, :]


def gather_body(where_ref, counts_ref, slab_ref, offsets_ref, final_ref, out_ref):
    chunks, comps, _ = slab_ref.shape
    n = counts_ref.shape[0]
    slots = NB_BLOCK // n
    block = where_ref[1]
    start = jnp.int32(0)
    for s in range(n):
        start = start + jnp.where(s < block, counts_ref[s], 0)
    count = counts_ref[block]
    row = lax.div(start, jnp.int32(n))
    shift = lax.rem(start, jnp.int32(n))
    lines = [offsets_ref[pl.ds(row + t, 1), :] for t in range(slots + 1)]
    at = iota((1, n), 1)
    wraps = at < shift
    base = jnp.where(wraps, at - shift + n, at - shift)
    wanted = [jnp.where(base + n * t < count, jnp.where(wraps, lines[t + 1], lines[t]), -1) for t in range(slots)]
    wanted = jnp.concatenate(wanted, axis=1)
    point = iota((LANES, slots * n), 0)
    picked = jnp.zeros((comps, slots * n), F32)
    for k in range(chunks):
        tile = slab_ref[k, :, :]
        final_ref[:, k * LANES:(k + 1) * LANES] = tile
        chosen = (point + k * LANES == wanted).astype(F32).astype(BF16)
        picked = picked + exact_dot(tile, chosen, ((1,), (0,)))
    rest = comps - LANES
    side = 2 * LANES
    picked = jnp.concatenate([picked, jnp.zeros((comps, side - slots * n), F32)], axis=1)
    picked = jnp.concatenate([picked, jnp.zeros((side - comps, side), F32)], axis=0)
    turned = picked.T
    tail = jnp.zeros((n, LANES), F32)
    for t in range(slots):
        out_ref[t, :, :] = turned[t * n:(t + 1) * n, 0:LANES]
        part = turned[t * n:(t + 1) * n, LANES:2 * LANES]
        tail = tail + (part if t == 0 else pltpu.roll(part, t * rest, 1))
    out_ref[slots, :, :] = tail


def relay_body(where_ref, counts_ref, column_ref, in_ref, out_ref, *, rest):
    n = counts_ref.shape[0]
    slots = NB_BLOCK // n
    share = in_ref.shape[0] - 1
    me = where_ref[1]
    column = column_ref[...]
    source_row = iota((n, n), 0)
    source_lane = iota((n, n), 1)
    wide = jnp.broadcast_to(column, (n, n))
    starts = jnp.sum(jnp.where(source_row < source_lane, wide, 0), axis=0, keepdims=True)
    counts = jnp.sum(jnp.where(source_row == source_lane, wide, 0), axis=0, keepdims=True)
    span = NB_BLOCK // 2
    window = jnp.where(source_row < n // 2, span * source_row + counts[:, 0:1], span * (source_row - n // 2))
    base = lax.rem(me - starts + 128 * n, jnp.int32(n))
    lane = iota((n, LANES), 1)
    heads = [jnp.zeros((n, LANES), F32) for _ in range(2)]
    tail = jnp.zeros((n, LANES), F32)
    for t in range(slots):
        position = base + n * t
        valid = position < counts
        inside = starts + position - window
        hit = jnp.logical_and(jnp.logical_and(inside >= 0, inside < span), valid)
        head = in_ref[t, :, :]
        part = in_ref[share, :, :]
        part = part if t == 0 else pltpu.roll(part, LANES - t * rest, 1)
        part = jnp.where(lane < rest, part, 0.0)
        for u in range(2):
            in_half = jnp.logical_and(hit, (inside < n) if u == 0 else (inside >= n))
            chosen = in_half.astype(F32).astype(BF16)
            heads[u] = heads[u] + exact_pick(chosen, head)
            tail = tail + exact_pick(chosen, part if u == 0 else pltpu.roll(part, u * rest, 1))
    for u in range(2):
        out_ref[u, :, :] = heads[u]
    out_ref[2, :, :] = tail


def settle_body(where_ref, counts_ref, in_ref, out_ref):
    comps, span = out_ref.shape
    n = in_ref.shape[1]
    rest = comps - LANES
    block = where_ref[1]
    device = iota((n, LANES), 0)
    at = iota((n, LANES), 1)
    window = jnp.where(block < n // 2, span * block + counts_ref[0], span * (block - n // 2))
    target = lax.rem(device - window + 256 * n, jnp.int32(n))
    total = None
    for u in range(2):
        chosen = (at == target + n * u).astype(F32).astype(BF16)
        tail = in_ref[2, :, :]
        tail = tail if u == 0 else pltpu.roll(tail, LANES - u * rest, 1)
        both = jnp.concatenate([in_ref[u, :, :], tail], axis=1).T
        value = exact_dot(both, chosen, ((1,), (0,)))
        total = value if total is None else total + value
    out_ref[...] = total[0:comps, 0:span]


def per_device(spectrum, courant, growth, quad_a, quad_b, sea_mask, nest_counts, nest_offsets):
    comps, points = spectrum.shape
    total = growth.shape[0]
    groups = lax.axis_size("comp")
    n = lax.axis_size("pts")
    chunks = points // LANES
    padded = 2 * LANES
    slab_rows = comps + 6
    sea_row = sea_mask.reshape(1, points)
    sea_tiles = sea_mask.reshape(chunks, LANES)
    where = jnp.stack([lax.axis_index("comp"), lax.axis_index("pts")]).astype(jnp.int32)
    edge = jax.ShapeDtypeStruct((8, padded), F32)

    up, down = call(edges_body, (edge, edge), 2)(spectrum, sea_row)
    before = lax.ppermute(up, "pts", [(i, i + 1) for i in range(n - 1)])
    after = lax.ppermute(down, "pts", [(i + 1, i) for i in range(n - 1)])
    slabs = call(pack_body, jax.ShapeDtypeStruct((chunks, slab_rows, LANES), F32), 5)(
        spectrum, sea_row, courant.reshape(1, comps), before, after
    )
    slabs = lax.all_to_all(slabs, "comp", split_axis=0, concat_axis=0, tiled=True)

    turned_a = quad_a.T
    result = call(
        steps_body,
        jax.ShapeDtypeStruct((groups, comps, LANES), F32),
        7,
        smem=(0,),
        scratch=(
            pltpu.VMEM((total, 2 * LANES), F32),
            pltpu.VMEM((total, LANES), F32),
            pltpu.VMEM((total, LANES), F32),
            pltpu.VMEM((total, LANES), F32),
        ),
    )(where, slabs, quad_a, quad_b, turned_a, growth.reshape(1, total), sea_tiles)
    result = lax.all_to_all(result, "comp", split_axis=0, concat_axis=0, tiled=True)

    slots = NB_BLOCK // n
    lines = jnp.pad(nest_offsets, (0, 4 * n)).reshape(-1, n)
    field, sent = call(
        gather_body,
        (jax.ShapeDtypeStruct((comps, points), F32), jax.ShapeDtypeStruct((slots + 1, n, LANES), F32)),
        4,
        smem=(0, 1),
    )(where, nest_counts, result, lines)
    sent = lax.all_to_all(sent.transpose(1, 0, 2), "pts", split_axis=0, concat_axis=0, tiled=True)
    sent = call(
        functools.partial(relay_body, rest=comps - LANES),
        jax.ShapeDtypeStruct((3, n, LANES), F32),
        4,
        smem=(0, 1),
    )(where, nest_counts, nest_counts.reshape(n, 1), sent.transpose(1, 0, 2))
    sent = lax.all_to_all(sent.transpose(1, 0, 2), "pts", split_axis=0, concat_axis=0, tiled=True)
    nest = call(settle_body, jax.ShapeDtypeStruct((comps, NB_BLOCK // 2), F32), 3, smem=(0, 1))(
        where, nest_counts, sent.transpose(1, 0, 2)
    )
    return (field, nest)


def solution(mesh):
    return jax.shard_map(
        per_device,
        mesh=mesh,
        in_specs=(P("comp", "pts"), P("comp"), P(), P(), P(), P("pts"), P(), P()),
        out_specs=(P("comp", "pts"), P("comp", "pts")),
        check_vma=False,
    )
```

```python
import functools

import jax
import jax.numpy as jnp
from jax import lax
from jax.experimental import pallas as pl
from jax.experimental.pallas import tpu as pltpu
from jax.sharding import PartitionSpec as P

STEPS = 2
LANES = 128
NB_BLOCK = 192
SLAB = 4
DISSIPATION = 0.5

F32 = jnp.float32
BF16 = jnp.bfloat16
VMEM = pl.BlockSpec(memory_space=pltpu.VMEM)
SMEM = pl.BlockSpec(memory_space=pltpu.SMEM)


def call(body, out_shape, n_in, smem=(), cost=None, scratch=(), vmem=8):
    specs = [SMEM if i in smem else VMEM for i in range(n_in)]
    outs = VMEM if not isinstance(out_shape, (tuple, list)) else tuple(VMEM for _ in out_shape)
    flops, bytes_accessed = cost or (1_000_000, 1_000_000)
    return pl.pallas_call(
        body,
        out_shape=out_shape,
        in_specs=specs,
        out_specs=outs,
        scratch_shapes=list(scratch),
        compiler_params=pltpu.CompilerParams(vmem_limit_bytes=vmem << 20),
        cost_estimate=pl.CostEstimate(flops=flops, bytes_accessed=bytes_accessed, transcendentals=0),
    )


def iota(shape, axis):
    return lax.broadcasted_iota(jnp.int32, shape, axis)


def split3(value):
    high = value.astype(BF16)
    rest = value - high.astype(F32)
    middle = rest.astype(BF16)
    low = (rest - middle.astype(F32)).astype(BF16)
    return high, middle, low


def exact_dot(value, chosen, dims):
    high, middle, low = (lax.dot_general(term, chosen, (dims, ((), ())), preferred_element_type=F32) for term in split3(value))
    return (high + middle) + low


def exact_pick(chosen, value):
    high, middle, low = (lax.dot_general(chosen, term, (((1,), (0,)), ((), ())), preferred_element_type=F32) for term in split3(value))
    return (high + middle) + low


def edges_body(field_ref, sea_ref, up_ref, down_ref):
    comps, points = field_ref.shape
    padded = up_ref.shape[1]
    for ref, start, order in ((up_ref, points - LANES, (LANES - 1, LANES - 2)), (down_ref, 0, (0, 1))):
        tile = field_ref[:, start:start + LANES]
        tile = jnp.concatenate([tile, jnp.zeros((padded - comps, LANES), F32)], axis=0)
        turned = tile.T
        for row, lane in enumerate(order):
            ref[row:row + 1, :] = turned[lane:lane + 1, :]
        sea = sea_ref[0:1, start + order[0]:start + order[0] + 1].astype(F32)
        ref[2:3, :] = jnp.broadcast_to(sea, (1, padded))
        ref[3:8, :] = jnp.zeros((5, padded), F32)


def pack_body(field_ref, sea_ref, courant_ref, before_ref, after_ref, out_ref):
    comps, points = field_ref.shape
    chunks = points // LANES
    padded = before_ref.shape[1]
    rows = jnp.concatenate(
        [before_ref[0:3, :], after_ref[0:3, :], jnp.concatenate([courant_ref[...], jnp.zeros((1, padded - comps), F32)], axis=1), jnp.zeros((1, padded), F32)],
        axis=0,
    )
    columns = rows.T[:comps, :]

    def wide(at):
        return jnp.broadcast_to(columns[:, at:at + 1], (comps, LANES))

    near_before, far_before, sea_before = wide(0), wide(1), wide(2)
    near_after, far_after, sea_after = wide(3), wide(4), wide(5)
    courant = wide(6)
    speed = jnp.abs(courant)
    stay = 1.0 - speed
    forward = courant > 0
    lane = iota((comps, LANES), 1)

    tiles = [field_ref[:, k * LANES:(k + 1) * LANES] for k in range(chunks)]
    ups = [pltpu.roll(tile, 1, 1) for tile in tiles]
    downs = [pltpu.roll(tile, LANES - 1, 1) for tile in tiles]
    moved = []
    for k in range(chunks):
        left = jnp.where(lane == 0, near_before if k == 0 else ups[k - 1], ups[k])
        right = jnp.where(lane == LANES - 1, near_after if k == chunks - 1 else downs[k + 1], downs[k])
        sea = sea_ref[0:1, k * LANES:(k + 1) * LANES].astype(F32)
        value = (stay * tiles[k] + speed * jnp.where(forward, left, right)) * sea
        out_ref[k, 0:comps, :] = value
        moved.append(value)

    first = jnp.broadcast_to(tiles[0][:, 0:1], (comps, LANES))
    last = jnp.broadcast_to(tiles[chunks - 1][:, LANES - 1:LANES], (comps, LANES))
    moved_before = (stay * near_before + speed * jnp.where(forward, far_before, first)) * sea_before
    moved_after = (stay * near_after + speed * jnp.where(forward, last, far_after)) * sea_after
    ghosts = courant
    for k in range(chunks):
        low = moved_before if k == 0 else pltpu.roll(moved[k - 1], k + 1, 1)
        high = moved_after if k == chunks - 1 else pltpu.roll(moved[k + 1], chunks + k, 1)
        ghosts = jnp.where(lane == k, low, jnp.where(lane == chunks + k, high, ghosts))
    turned = jnp.concatenate([ghosts, jnp.zeros((padded - comps, LANES), F32)], axis=0).T
    for k in range(chunks):
        for at, source in ((0, k), (2, chunks + k), (4, 2 * chunks)):
            out_ref[k, comps + at:comps + at + 1, :] = turned[source:source + 1, 0:LANES]
            out_ref[k, comps + at + 1:comps + at + 2, :] = turned[source:source + 1, LANES:2 * LANES]


def steps_body(where_ref, slab_ref, a_ref, b_ref, turned_a_ref, growth_ref, sea_ref, out_ref, moved_ref, courant_ref, gain_ref, result_ref):
    groups, _, _ = slab_ref.shape
    comps = out_ref.shape[1]
    total = moved_ref.shape[0]
    lane = iota((comps, LANES), 1)
    for g in range(groups):
        start = g * comps
        moved_ref[start:start + comps, 0:LANES] = slab_ref[g, 0:comps, :]
        extra = slab_ref[g, comps:comps + 6, :]
        rows = jnp.concatenate([extra, jnp.zeros((2, LANES), F32)], axis=0)
        columns = rows.T
        tall = [jnp.concatenate([columns[:, 2 * i:2 * i + 1], columns[:comps - LANES, 2 * i + 1:2 * i + 2]], axis=0) for i in range(3)]
        low, high, courant = (jnp.broadcast_to(t, (comps, LANES)) for t in tall)
        moved_ref[start:start + comps, LANES:2 * LANES] = jnp.where(lane == 0, high, jnp.where(lane == LANES - 1, low, 0.0))
        courant_ref[start:start + comps, :] = courant
    growth = growth_ref[...]
    width = growth.shape[1]
    gain_ref[...] = jnp.broadcast_to(jnp.broadcast_to(growth, (8, width)).T[:, 0:1], (total, LANES))

    def source(moved, gain):
        rounded = moved.astype(BF16)
        left = jnp.dot(a_ref[...], rounded, preferred_element_type=F32)
        right = jnp.dot(b_ref[...], rounded, preferred_element_type=F32)
        pairs = (left * right).astype(BF16)
        transfer = jnp.dot(turned_a_ref[...], pairs, preferred_element_type=F32)
        mean = jnp.sum(moved * moved, axis=0, keepdims=True) / total
        spread = jnp.sqrt(mean + 1e-06)
        scale = 1.0 / (1.0 + DISSIPATION * spread)
        return (moved + gain * moved + transfer) * scale

    gain = gain_ref[...]
    moved = moved_ref[...]
    field = source(moved, jnp.concatenate([gain, gain], axis=1))
    left = pltpu.roll(field, 1, 1)[:, 0:LANES]
    right = pltpu.roll(field, 2 * LANES - 1, 1)[:, 0:LANES]
    courant = courant_ref[...]
    speed = jnp.abs(courant)
    sea = sea_ref[pl.ds(where_ref[0], 1), :].astype(F32)
    moved = ((1.0 - speed) * field[:, 0:LANES] + speed * jnp.where(courant > 0, left, right)) * sea
    result_ref[...] = source(moved, gain)
    for g in range(groups):
        out_ref[g, :, :] = result_ref[g * comps:(g + 1) * comps, :]


def gather_body(where_ref, counts_ref, slab_ref, offsets_ref, out_ref):
    chunks, comps, _ = slab_ref.shape
    n = counts_ref.shape[0]
    rows = SLAB * n
    slots = NB_BLOCK // n
    block = where_ref[1]
    start = jnp.int32(0)
    for s in range(n):
        start = start + jnp.where(s < block, counts_ref[s], 0)
    count = counts_ref[block]
    row = lax.div(start, jnp.int32(n))
    shift = lax.rem(start, jnp.int32(n))
    lines = [offsets_ref[pl.ds(row + t, 1), :] for t in range(slots + 1)]
    lane = iota((1, rows), 1)
    at = lane // SLAB
    slot = lane % SLAB
    wraps = at < shift
    base = jnp.where(wraps, at - shift + n, at - shift)
    wanted = jnp.full((1, rows), -1, jnp.int32)
    for t in range(slots):
        mine = jnp.logical_and(slot == t, base + n * t < count)
        wanted = jnp.where(mine, jnp.where(wraps, lines[t + 1], lines[t]), wanted)
    point = iota((LANES, rows), 0)
    picked = jnp.zeros((comps, rows), F32)
    for k in range(chunks):
        chosen = (point + k * LANES == wanted).astype(F32).astype(BF16)
        picked = picked + exact_dot(slab_ref[k, :, :], chosen, ((1,), (0,)))
    side = 2 * LANES
    turned = jnp.concatenate([picked, jnp.zeros((side - comps, rows), F32)], axis=0).T
    out_ref[...] = fold(turned, slots, comps - LANES)


def fold(turned, slots, rest):
    rows = turned.shape[0]
    slot = iota((rows, LANES), 0) % SLAB
    lane = iota((rows, LANES), 1)
    main = turned[:, 0:LANES]
    side = turned[:, LANES:2 * LANES]
    out = jnp.where(slot < slots, main, 0.0)
    for t in range(slots):
        part = pltpu.roll(side, slots - t, 0)
        part = part if t == 0 else pltpu.roll(part, t * rest, 1)
        inside = jnp.logical_and(lane >= t * rest, lane < (t + 1) * rest)
        out = jnp.where(jnp.logical_and(slot == slots, inside), part, out)
    return out


def unfold(value, slots, rest):
    rows = value.shape[0]
    slot = iota((rows, LANES), 0) % SLAB
    lane = iota((rows, LANES), 1)
    side = jnp.zeros((rows, LANES), F32)
    for t in range(slots):
        part = pltpu.roll(value, rows - (slots - t), 0)
        part = part if t == 0 else pltpu.roll(part, LANES - t * rest, 1)
        side = jnp.where(jnp.logical_and(slot == t, lane < rest), part, side)
    return jnp.concatenate([jnp.where(slot < slots, value, 0.0), side], axis=1)


def relay_body(where_ref, column_ref, in_ref, out_ref, *, rest):
    rows = in_ref.shape[0]
    n = rows // SLAB
    slots = NB_BLOCK // n
    me = where_ref[1]
    row = iota((rows, rows), 0)
    lane = iota((rows, rows), 1)
    wide = jnp.broadcast_to(column_ref[...], (n, rows))
    source = iota((n, rows), 0)
    target = iota((n, rows), 1) // SLAB
    starts = jnp.sum(jnp.where(source < target, wide, 0), axis=0, keepdims=True)
    counts = jnp.sum(jnp.where(source == target, wide, 0), axis=0, keepdims=True)
    span = NB_BLOCK // 2
    slot = iota((1, rows), 1) % SLAB
    position = lax.rem(me - starts + 128 * n, jnp.int32(n)) + n * slot
    valid = jnp.logical_and(position < counts, slot < slots)
    entry = jnp.where(valid, starts + position, -(1 << 20))
    place = iota((rows, 1), 0)
    half = place % SLAB
    place = place // SLAB
    window = jnp.where(place < n // 2, span * place + counts[:, 0:1], span * (place - n // 2)) + n * half
    size = jnp.where(half == 0, n, jnp.where(half == 1, span - n, 0))
    inside = entry - window
    chosen = jnp.logical_and(inside >= 0, inside < size).astype(F32).astype(BF16)
    value = exact_pick(chosen, unfold(in_ref[...], slots, rest))
    out_ref[...] = fold(value, 2, rest)


def settle_body(where_ref, counts_ref, in_ref, out_ref):
    comps, span = out_ref.shape
    rows = in_ref.shape[0]
    n = rows // SLAB
    block = where_ref[1]
    row = iota((rows, LANES), 0)
    device = row // SLAB
    half = row % SLAB
    at = iota((rows, LANES), 1)
    window = jnp.where(block < n // 2, span * block + counts_ref[0], span * (block - n // 2))
    target = lax.rem(device - window + 256 * n, jnp.int32(n)) + n * half
    chosen = jnp.logical_and(at == target, half < 2).astype(F32).astype(BF16)
    value = exact_dot(unfold(in_ref[...], 2, comps - LANES).T, chosen, ((1,), (0,)))
    out_ref[...] = value[0:comps, 0:span]


def per_device(spectrum, courant, growth, quad_a, quad_b, sea_mask, nest_counts, nest_offsets):
    comps, points = spectrum.shape
    total = growth.shape[0]
    groups = lax.axis_size("comp")
    n = lax.axis_size("pts")
    chunks = points // LANES
    padded = 2 * LANES
    slab_rows = comps + 6
    sea_row = sea_mask.reshape(1, points)
    sea_tiles = sea_mask.reshape(chunks, LANES)
    where = jnp.stack([lax.axis_index("comp"), lax.axis_index("pts")]).astype(jnp.int32)
    edge = jax.ShapeDtypeStruct((8, padded), F32)

    up, down = call(edges_body, (edge, edge), 2)(spectrum, sea_row)
    before = lax.ppermute(up, "pts", [(i, i + 1) for i in range(n - 1)])
    after = lax.ppermute(down, "pts", [(i + 1, i) for i in range(n - 1)])
    slabs = call(pack_body, jax.ShapeDtypeStruct((chunks, slab_rows, LANES), F32), 5)(
        spectrum, sea_row, courant.reshape(1, comps), before, after
    )
    slabs = lax.all_to_all(slabs, "comp", split_axis=0, concat_axis=0, tiled=True)

    turned_a = quad_a.T
    result = call(
        steps_body,
        jax.ShapeDtypeStruct((groups, comps, LANES), F32),
        7,
        smem=(0,),
        scratch=(
            pltpu.VMEM((total, 2 * LANES), F32),
            pltpu.VMEM((total, LANES), F32),
            pltpu.VMEM((total, LANES), F32),
            pltpu.VMEM((total, LANES), F32),
        ),
        vmem=28,
    )(where, slabs, quad_a, quad_b, turned_a, growth.reshape(1, total), sea_tiles)
    result = lax.all_to_all(result, "comp", split_axis=0, concat_axis=0, tiled=True)

    lines = jnp.repeat(jnp.pad(nest_offsets, (0, 4 * n)).reshape(-1, n), SLAB, axis=1)
    slab = jax.ShapeDtypeStruct((SLAB * n, LANES), F32)
    sent = call(gather_body, slab, 4, smem=(0, 1))(where, nest_counts, result, lines)
    sent = lax.all_to_all(sent, "pts", split_axis=0, concat_axis=0, tiled=True)
    field = result.transpose(1, 0, 2).reshape(comps, points)
    sent = call(functools.partial(relay_body, rest=comps - LANES), slab, 3, smem=(0,))(where, nest_counts.reshape(n, 1), sent)
    sent = lax.all_to_all(sent, "pts", split_axis=0, concat_axis=0, tiled=True)
    nest = call(settle_body, jax.ShapeDtypeStruct((comps, NB_BLOCK // 2), F32), 3, smem=(0, 1))(where, nest_counts, sent)
    return (field, nest)


def solution(mesh):
    return jax.shard_map(
        per_device,
        mesh=mesh,
        in_specs=(P("comp", "pts"), P("comp"), P(), P(), P(), P("pts"), P(), P()),
        out_specs=(P("comp", "pts"), P("comp", "pts")),
        check_vma=False,
    )
```

```python
import functools

import jax
import jax.numpy as jnp
from jax import lax
from jax.experimental import pallas as pl
from jax.experimental.pallas import tpu as pltpu
from jax.sharding import PartitionSpec as P

STEPS = 2
LANES = 128
NB_BLOCK = 192
SLAB = 4
DISSIPATION = 0.5

F32 = jnp.float32
BF16 = jnp.bfloat16
VMEM = pl.BlockSpec(memory_space=pltpu.VMEM)
HBM = pl.BlockSpec(memory_space=pltpu.HBM)


def call(body, out_shape, ins, outs=VMEM, scratch=(), vmem=8):
    return pl.pallas_call(
        body,
        out_shape=out_shape,
        in_specs=list(ins),
        out_specs=outs,
        scratch_shapes=list(scratch),
        compiler_params=pltpu.CompilerParams(vmem_limit_bytes=vmem << 20),
        cost_estimate=pl.CostEstimate(flops=1_000_000, bytes_accessed=1_000_000, transcendentals=0),
    )


def iota(shape, axis):
    return lax.broadcasted_iota(jnp.int32, shape, axis)


def split3(value):
    high = value.astype(BF16)
    rest = value - high.astype(F32)
    middle = rest.astype(BF16)
    low = (rest - middle.astype(F32)).astype(BF16)
    return high, middle, low


def exact_dot(value, chosen, dims):
    high, middle, low = (lax.dot_general(term, chosen, (dims, ((), ())), preferred_element_type=F32) for term in split3(value))
    return (high + middle) + low


def exact_pick(chosen, value):
    high, middle, low = (lax.dot_general(chosen, term, (((1,), (0,)), ((), ())), preferred_element_type=F32) for term in split3(value))
    return (high + middle) + low


def edges_body(field_ref, side_ref, up_ref, down_ref):
    comps, points = field_ref.shape
    padded = up_ref.shape[1]
    for ref, start, order in ((up_ref, points - LANES, (LANES - 1, LANES - 2)), (down_ref, 0, (0, 1))):
        tile = jnp.concatenate([field_ref[:, start:start + LANES], jnp.zeros((padded - comps, LANES), F32)], axis=0)
        turned = tile.T
        for row, lane in enumerate(order):
            ref[row:row + 1, :] = turned[lane:lane + 1, :]
        point = start + order[0]
        ref[2:3, :] = jnp.broadcast_to(side_ref[0:1, point:point + 1], (1, padded))
        ref[3:8, :] = jnp.zeros((5, padded), F32)


STEP = 40


def pack_body(field_ref, side_ref, before_ref, after_ref, out_ref, slab_ref, sems):
    comps, points = field_ref.shape
    chunks = points // LANES
    padded = before_ref.shape[1]
    whole = comps // 8 * 8
    rows = jnp.concatenate([before_ref[0:3, :], after_ref[0:3, :], side_ref[1:2, 0:padded], jnp.zeros((1, padded), F32)], axis=0)
    columns = rows.T[:comps, :]

    def wide(at):
        return jnp.broadcast_to(columns[:, at:at + 1], (comps, LANES))

    near_before, far_before, sea_before = wide(0), wide(1), wide(2)
    near_after, far_after, sea_after = wide(3), wide(4), wide(5)
    courant = wide(6)
    speed = jnp.abs(courant)
    stay = 1.0 - speed
    forward = courant > 0
    lane = iota((comps, LANES), 1)

    tiles = [field_ref[:, k * LANES:(k + 1) * LANES] for k in range(chunks)]
    ups = [pltpu.roll(tile, 1, 1) for tile in tiles]
    downs = [pltpu.roll(tile, LANES - 1, 1) for tile in tiles]
    moved = []
    copies = []
    for k in range(chunks):
        left = jnp.where(lane == 0, near_before if k == 0 else ups[k - 1], ups[k])
        right = jnp.where(lane == LANES - 1, near_after if k == chunks - 1 else downs[k + 1], downs[k])
        sea = side_ref[0:1, k * LANES:(k + 1) * LANES]
        value = (stay * tiles[k] + speed * jnp.where(forward, left, right)) * sea
        slab_ref[k, 0:comps, :] = value
        moved.append(value)

    first = jnp.broadcast_to(tiles[0][:, 0:1], (comps, LANES))
    last = jnp.broadcast_to(tiles[chunks - 1][:, LANES - 1:LANES], (comps, LANES))
    moved_before = (stay * near_before + speed * jnp.where(forward, far_before, first)) * sea_before
    moved_after = (stay * near_after + speed * jnp.where(forward, last, far_after)) * sea_after
    ghosts = courant
    for k in range(chunks):
        low = moved_before if k == 0 else pltpu.roll(moved[k - 1], k + 1, 1)
        high = moved_after if k == chunks - 1 else pltpu.roll(moved[k + 1], chunks + k, 1)
        ghosts = jnp.where(lane == k, low, jnp.where(lane == chunks + k, high, ghosts))
    turned = jnp.concatenate([ghosts, jnp.zeros((padded - comps, LANES), F32)], axis=0).T
    head = turned[0:3 * chunks, 0:LANES]
    tail = turned[0:3 * chunks, LANES:2 * LANES]
    mixed = tail[0:chunks] + pltpu.roll(tail[chunks:2 * chunks], STEP, 1) + pltpu.roll(tail[2 * chunks:3 * chunks], 2 * STEP, 1)
    for k in range(chunks):
        slab_ref[k, comps:comps + 1, :] = head[k:k + 1]
        slab_ref[k, comps + 1:comps + 2, :] = head[chunks + k:chunks + k + 1]
        slab_ref[k, comps + 2:comps + 3, :] = head[2 * chunks:2 * chunks + 1]
        slab_ref[k, comps + 3:comps + 4, :] = mixed[k:k + 1]
        slab_ref[k, comps + 4:comps + 5, :] = side_ref[0:1, k * LANES:(k + 1) * LANES]
        slab_ref[k, comps + 5:comps + 6, :] = jnp.zeros((1, LANES), F32)
        copy = pltpu.make_async_copy(slab_ref.at[k], out_ref.at[k], sems.at[k])
        copy.start()
        copies.append(copy)
    for copy in copies:
        copy.wait()


def stack_body(a_ref, b_ref, out_ref):
    half = a_ref.shape[1]
    for at, ref in ((0, a_ref), (half, b_ref)):
        for start in range(0, half, LANES):
            out_ref[at + start:at + start + LANES, :] = ref[:, start:start + LANES].T


def steps_body(packed_ref, stacked_ref, turned_ref, growth_ref, out_ref, slab_ref, both_ref, turned_a_ref, moved_ref, courant_ref, gain_ref, result_ref, sems):
    groups, rows, _ = slab_ref.shape
    comps = rows - 6
    total = moved_ref.shape[0]
    half = both_ref.shape[0] // 2
    rest = comps - LANES
    packed = pltpu.make_async_copy(packed_ref, slab_ref, sems.at[groups])
    stacked = pltpu.make_async_copy(stacked_ref, both_ref, sems.at[groups + 1])
    turned = pltpu.make_async_copy(turned_ref, turned_a_ref, sems.at[groups + 2])
    for copy in (packed, stacked, turned):
        copy.start()
    packed.wait()
    lane = iota((comps, LANES), 1)
    columns = jnp.concatenate([slab_ref[g, rows - 8:rows, :] for g in range(groups)] + [jnp.zeros((LANES - 8 * groups, LANES), F32)], axis=0).T
    for g in range(groups):
        start = g * comps
        moved_ref[start:start + comps, 0:LANES] = slab_ref[g, 0:comps, :]
        at = 8 * g + 2
        low, high, courant = (
            jnp.broadcast_to(jnp.concatenate([columns[:, at + i:at + i + 1], columns[STEP * i:STEP * i + rest, at + 3:at + 4]], axis=0), (comps, LANES))
            for i in range(3)
        )
        moved_ref[start:start + comps, LANES:2 * LANES] = jnp.where(lane == 0, low, jnp.where(lane == LANES - 1, high, 0.0))
        courant_ref[start:start + comps, :] = courant
    growth = growth_ref[...]
    width = growth.shape[1]
    gain_ref[...] = jnp.broadcast_to(jnp.broadcast_to(growth, (8, width)).T[:, 0:1], (total, LANES))

    def source(moved, gain):
        rounded = moved.astype(BF16)
        both = jnp.dot(both_ref[...], rounded, preferred_element_type=F32)
        pairs = (both[0:half] * both[half:2 * half]).astype(BF16)
        transfer = jnp.dot(turned_a_ref[...], pairs, preferred_element_type=F32)
        mean = jnp.sum(moved * moved, axis=0, keepdims=True) / total
        spread = jnp.sqrt(mean + 1e-06)
        scale = 1.0 / (1.0 + DISSIPATION * spread)
        return (moved + gain * moved + transfer) * scale

    gain = gain_ref[...]
    moved = moved_ref[...]
    stacked.wait()
    turned.wait()
    field = source(moved, jnp.concatenate([gain, gain], axis=1))
    field, ghost = field[:, 0:LANES], field[:, LANES:2 * LANES]
    lane = iota((total, LANES), 1)
    left = jnp.where(lane == 0, ghost, pltpu.roll(field, 1, 1))
    right = jnp.where(lane == LANES - 1, ghost, pltpu.roll(field, LANES - 1, 1))
    courant = courant_ref[...]
    speed = jnp.abs(courant)
    sea = slab_ref[0, rows - 2:rows - 1, :]
    moved = ((1.0 - speed) * field + speed * jnp.where(courant > 0, left, right)) * sea
    value = source(moved, gain)
    copies = []
    for g in range(groups):
        result_ref[g, :, :] = value[g * comps:(g + 1) * comps]
        copy = pltpu.make_async_copy(result_ref.at[g], out_ref.at[g], sems.at[g])
        copy.start()
        copies.append(copy)
    for copy in copies:
        copy.wait()


def gather_body(block_ref, column_ref, slab_ref, offsets_ref, out_ref):
    chunks, comps, _ = slab_ref.shape
    n = column_ref.shape[0]
    rows = SLAB * n
    slots = NB_BLOCK // n
    block = block_ref[0:1, 0:1]
    device = iota((n, 1), 0)
    start = jnp.sum(jnp.where(device < block, column_ref[...], 0), axis=0, keepdims=True)
    count = jnp.sum(jnp.where(device == block, column_ref[...], 0), axis=0, keepdims=True)
    shift = lax.rem(start, jnp.int32(n))
    lane = iota((1, rows), 1)
    at = lane // SLAB
    slot = lane % SLAB
    wraps = at < shift
    base = jnp.where(wraps, at - shift + n, at - shift)
    line = lax.div(start, jnp.int32(n)) + slot + jnp.where(wraps, 1, 0)
    table = offsets_ref[...]
    wanted = jnp.sum(jnp.where(iota(table.shape, 0) == line, table, 0), axis=0, keepdims=True)
    wanted = jnp.where(jnp.logical_and(slot < slots, base + n * slot < count), wanted, -1)
    point = iota((LANES, rows), 0)
    picked = jnp.zeros((comps, rows), F32)
    for k in range(chunks):
        chosen = (point + k * LANES == wanted).astype(F32).astype(BF16)
        picked = picked + exact_dot(slab_ref[k, :, :], chosen, ((1,), (0,)))
    side = 2 * LANES
    turned = jnp.concatenate([picked, jnp.zeros((side - comps, rows), F32)], axis=0).T
    out_ref[...] = fold(turned, slots, comps - LANES)


def fold(turned, slots, rest):
    rows = turned.shape[0]
    slot = iota((rows, LANES), 0) % SLAB
    lane = iota((rows, LANES), 1)
    main = turned[:, 0:LANES]
    side = turned[:, LANES:2 * LANES]
    out = jnp.where(slot < slots, main, 0.0)
    for t in range(slots):
        part = pltpu.roll(side, slots - t, 0)
        part = part if t == 0 else pltpu.roll(part, t * rest, 1)
        inside = jnp.logical_and(lane >= t * rest, lane < (t + 1) * rest)
        out = jnp.where(jnp.logical_and(slot == slots, inside), part, out)
    return out


def unfold(value, slots, rest):
    rows = value.shape[0]
    slot = iota((rows, LANES), 0) % SLAB
    lane = iota((rows, LANES), 1)
    side = jnp.zeros((rows, LANES), F32)
    for t in range(slots):
        part = pltpu.roll(value, rows - (slots - t), 0)
        part = part if t == 0 else pltpu.roll(part, LANES - t * rest, 1)
        side = jnp.where(jnp.logical_and(slot == t, lane < rest), part, side)
    return jnp.concatenate([jnp.where(slot < slots, value, 0.0), side], axis=1)


def relay_body(block_ref, column_ref, in_ref, out_ref, *, rest):
    rows = in_ref.shape[0]
    n = rows // SLAB
    slots = NB_BLOCK // n
    me = block_ref[0:1, 0:1]
    wide = jnp.broadcast_to(column_ref[...], (n, rows))
    source = iota((n, rows), 0)
    target = iota((n, rows), 1) // SLAB
    starts = jnp.sum(jnp.where(source < target, wide, 0), axis=0, keepdims=True)
    counts = jnp.sum(jnp.where(source == target, wide, 0), axis=0, keepdims=True)
    span = NB_BLOCK // 2
    slot = iota((1, rows), 1) % SLAB
    position = lax.rem(me - starts + 128 * n, jnp.int32(n)) + n * slot
    valid = jnp.logical_and(position < counts, slot < slots)
    entry = jnp.where(valid, starts + position, -(1 << 20))
    place = iota((rows, 1), 0)
    half = place % SLAB
    place = place // SLAB
    window = jnp.where(place < n // 2, span * place + counts[:, 0:1], span * (place - n // 2)) + n * half
    size = jnp.where(half == 0, n, jnp.where(half == 1, span - n, 0))
    inside = entry - window
    chosen = jnp.logical_and(inside >= 0, inside < size).astype(F32).astype(BF16)
    value = exact_pick(chosen, unfold(in_ref[...], slots, rest))
    out_ref[...] = fold(value, 2, rest)


def settle_body(block_ref, column_ref, in_ref, out_ref):
    comps, span = out_ref.shape
    rows = in_ref.shape[0]
    n = rows // SLAB
    block = block_ref[0:1, 0:1]
    row = iota((rows, LANES), 0)
    device = row // SLAB
    half = row % SLAB
    at = iota((rows, LANES), 1)
    window = jnp.where(block < n // 2, span * block + column_ref[0:1, 0:1], span * (block - n // 2))
    target = lax.rem(device - window + 256 * n, jnp.int32(n)) + n * half
    chosen = jnp.logical_and(at == target, half < 2).astype(F32).astype(BF16)
    value = exact_dot(unfold(in_ref[...], 2, comps - LANES).T, chosen, ((1,), (0,)))
    out_ref[...] = value[0:comps, 0:span]


def per_device(spectrum, courant, growth, quad_a, quad_b, sea_mask, nest_counts, nest_offsets):
    comps, points = spectrum.shape
    total = growth.shape[0]
    groups = lax.axis_size("comp")
    n = lax.axis_size("pts")
    chunks = points // LANES
    padded = 2 * LANES
    packed = jax.ShapeDtypeStruct((chunks, comps + 6, LANES), F32)
    edge = jax.ShapeDtypeStruct((8, padded), F32)
    slab = jax.ShapeDtypeStruct((SLAB * n, LANES), F32)

    side = jnp.concatenate([sea_mask.astype(F32), courant, jnp.zeros((points - comps,), F32)]).reshape(2, points)
    up, down = call(edges_body, (edge, edge), (VMEM, VMEM), (VMEM, VMEM))(spectrum, side)
    before = lax.ppermute(up, "pts", [(i, i + 1) for i in range(n - 1)])
    after = lax.ppermute(down, "pts", [(i + 1, i) for i in range(n - 1)])
    slabs = call(
        pack_body, packed, (VMEM,) * 4, HBM, scratch=(pltpu.VMEM(packed.shape, F32), pltpu.SemaphoreType.DMA((chunks,)))
    )(spectrum, side, before, after)
    slabs = lax.all_to_all(slabs, "comp", split_axis=0, concat_axis=0, tiled=True)

    both = call(stack_body, jax.ShapeDtypeStruct((2 * quad_a.shape[0], total), BF16), (VMEM, VMEM), vmem=16)(quad_a.T, quad_b.T)
    result = call(
        steps_body,
        jax.ShapeDtypeStruct((groups, comps, LANES), F32),
        (HBM, HBM, HBM, VMEM),
        HBM,
        scratch=(
            pltpu.VMEM(packed.shape, F32),
            pltpu.VMEM((2 * quad_a.shape[0], total), BF16),
            pltpu.VMEM((total, quad_a.shape[0]), BF16),
            pltpu.VMEM((total, 2 * LANES), F32),
            pltpu.VMEM((total, LANES), F32),
            pltpu.VMEM((total, LANES), F32),
            pltpu.VMEM((groups, comps, LANES), F32),
            pltpu.SemaphoreType.DMA((groups + 3,)),
        ),
        vmem=58,
    )(slabs, both, quad_a.T, growth.reshape(1, total))
    result = lax.all_to_all(result, "comp", split_axis=0, concat_axis=0, tiled=True)

    block = jnp.full((1, LANES), lax.axis_index("pts"), jnp.int32)
    column = nest_counts.reshape(n, 1)
    lines = jnp.repeat(jnp.pad(nest_offsets, (0, 4 * n)).reshape(-1, n), SLAB, axis=1)
    sent = call(gather_body, slab, (VMEM,) * 4)(block, column, result, lines)
    sent = lax.all_to_all(sent, "pts", split_axis=0, concat_axis=0, tiled=True)
    field = result.transpose(1, 0, 2).reshape(comps, points)
    sent = call(functools.partial(relay_body, rest=comps - LANES), slab, (VMEM,) * 3)(block, column, sent)
    sent = lax.all_to_all(sent, "pts", split_axis=0, concat_axis=0, tiled=True)
    nest = call(settle_body, jax.ShapeDtypeStruct((comps, NB_BLOCK // 2), F32), (VMEM,) * 3)(block, column, sent)
    return (field, nest)


def solution(mesh):
    return jax.shard_map(
        per_device,
        mesh=mesh,
        in_specs=(P("comp", "pts"), P("comp"), P(), P(), P(), P("pts"), P(), P()),
        out_specs=(P("comp", "pts"), P("comp", "pts")),
        check_vma=False,
    )
```

```python
import functools

import jax
import jax.numpy as jnp
from jax import lax
from jax.experimental import pallas as pl
from jax.experimental.pallas import tpu as pltpu
from jax.sharding import PartitionSpec as P

STEPS = 2
LANES = 128
NB_BLOCK = 192
SLAB = 4
BLOCK = 336
DISSIPATION = 0.5

F32 = jnp.float32
BF16 = jnp.bfloat16
VMEM = pl.BlockSpec(memory_space=pltpu.VMEM)
HBM = pl.BlockSpec(memory_space=pltpu.HBM)


def call(body, out_shape, ins, outs=VMEM, scratch=(), vmem=8):
    return pl.pallas_call(
        body,
        out_shape=out_shape,
        in_specs=list(ins),
        out_specs=outs,
        scratch_shapes=list(scratch),
        compiler_params=pltpu.CompilerParams(vmem_limit_bytes=vmem << 20),
        cost_estimate=pl.CostEstimate(flops=1_000_000, bytes_accessed=1_000_000, transcendentals=0),
    )


def iota(shape, axis):
    return lax.broadcasted_iota(jnp.int32, shape, axis)


def split3(value):
    high = value.astype(BF16)
    rest = value - high.astype(F32)
    middle = rest.astype(BF16)
    low = (rest - middle.astype(F32)).astype(BF16)
    return high, middle, low


def exact_dot(value, chosen, dims):
    high, middle, low = (lax.dot_general(term, chosen, (dims, ((), ())), preferred_element_type=F32) for term in split3(value))
    return (high + middle) + low


def exact_pick(chosen, value):
    high, middle, low = (lax.dot_general(chosen, term, (((1,), (0,)), ((), ())), preferred_element_type=F32) for term in split3(value))
    return (high + middle) + low


def edges_body(field_ref, side_ref, up_ref, down_ref):
    comps, points = field_ref.shape
    padded = up_ref.shape[1]
    for ref, start, order in ((up_ref, points - LANES, (LANES - 1, LANES - 2)), (down_ref, 0, (0, 1))):
        tile = jnp.concatenate([field_ref[:, start:start + LANES], jnp.zeros((padded - comps, LANES), F32)], axis=0)
        turned = tile.T
        for row, lane in enumerate(order):
            ref[row:row + 1, :] = turned[lane:lane + 1, :]
        point = start + order[0]
        ref[2:3, :] = jnp.broadcast_to(side_ref[0:1, point:point + 1], (1, padded))
        ref[3:8, :] = jnp.zeros((5, padded), F32)


STEP = 40


def pack_body(field_ref, side_ref, before_ref, after_ref, out_ref, slab_ref, sems):
    comps, points = field_ref.shape
    chunks = points // LANES
    padded = before_ref.shape[1]
    whole = comps // 8 * 8
    rows = jnp.concatenate([before_ref[0:3, :], after_ref[0:3, :], side_ref[1:2, 0:padded], jnp.zeros((1, padded), F32)], axis=0)
    columns = rows.T[:comps, :]

    def wide(at):
        return jnp.broadcast_to(columns[:, at:at + 1], (comps, LANES))

    near_before, far_before, sea_before = wide(0), wide(1), wide(2)
    near_after, far_after, sea_after = wide(3), wide(4), wide(5)
    courant = wide(6)
    speed = jnp.abs(courant)
    stay = 1.0 - speed
    forward = courant > 0
    lane = iota((comps, LANES), 1)

    tiles = [field_ref[:, k * LANES:(k + 1) * LANES] for k in range(chunks)]
    ups = [pltpu.roll(tile, 1, 1) for tile in tiles]
    downs = [pltpu.roll(tile, LANES - 1, 1) for tile in tiles]
    moved = []
    copies = []
    for k in range(chunks):
        left = jnp.where(lane == 0, near_before if k == 0 else ups[k - 1], ups[k])
        right = jnp.where(lane == LANES - 1, near_after if k == chunks - 1 else downs[k + 1], downs[k])
        sea = side_ref[0:1, k * LANES:(k + 1) * LANES]
        value = (stay * tiles[k] + speed * jnp.where(forward, left, right)) * sea
        slab_ref[k, 0:comps, :] = value
        moved.append(value)

    first = jnp.broadcast_to(tiles[0][:, 0:1], (comps, LANES))
    last = jnp.broadcast_to(tiles[chunks - 1][:, LANES - 1:LANES], (comps, LANES))
    moved_before = (stay * near_before + speed * jnp.where(forward, far_before, first)) * sea_before
    moved_after = (stay * near_after + speed * jnp.where(forward, last, far_after)) * sea_after
    ghosts = courant
    for k in range(chunks):
        low = moved_before if k == 0 else pltpu.roll(moved[k - 1], k + 1, 1)
        high = moved_after if k == chunks - 1 else pltpu.roll(moved[k + 1], chunks + k, 1)
        ghosts = jnp.where(lane == k, low, jnp.where(lane == chunks + k, high, ghosts))
    turned = jnp.concatenate([ghosts, jnp.zeros((padded - comps, LANES), F32)], axis=0).T
    head = turned[0:3 * chunks, 0:LANES]
    tail = turned[0:3 * chunks, LANES:2 * LANES]
    mixed = tail[chunks:2 * chunks] + pltpu.roll(tail[0:chunks], STEP, 1) + pltpu.roll(tail[2 * chunks:3 * chunks], 2 * STEP, 1)
    for k in range(chunks):
        slab_ref[k, comps:comps + 1, :] = head[chunks + k:chunks + k + 1]
        slab_ref[k, comps + 1:comps + 2, :] = head[k:k + 1]
        slab_ref[k, comps + 2:comps + 3, :] = head[2 * chunks:2 * chunks + 1]
        slab_ref[k, comps + 3:comps + 4, :] = mixed[k:k + 1]
        slab_ref[k, comps + 4:comps + 5, :] = side_ref[0:1, k * LANES:(k + 1) * LANES]
        slab_ref[k, comps + 5:comps + 6, :] = jnp.zeros((1, LANES), F32)
        copy = pltpu.make_async_copy(slab_ref.at[k], out_ref.at[k], sems.at[k])
        copy.start()
        copies.append(copy)
    for copy in copies:
        copy.wait()


def stack_body(a_ref, b_ref, growth_ref, both_ref, turned_ref, gain_ref, *, comps):
    total, half = a_ref.shape
    rows = comps + 6
    groups = total // comps
    gap = jnp.zeros((rows - comps, half), F32)
    for at, ref in ((0, a_ref), (half, b_ref)):
        whole = ref[...].astype(F32)
        spread = jnp.concatenate([part for g in range(groups) for part in (whole[g * comps:(g + 1) * comps], gap)], axis=0)
        if at == 0:
            turned_ref[...] = spread.astype(BF16)
        for start in range(0, half, LANES):
            both_ref[at + start:at + start + LANES, :] = spread[:, start:start + LANES].T.astype(BF16)
    growth = growth_ref[...]
    column = jnp.broadcast_to(growth, (8, total)).T[:, 0:1]
    for g in range(groups):
        gain_ref[g * rows:g * rows + comps, :] = jnp.broadcast_to(column[g * comps:(g + 1) * comps], (comps, LANES))
        gain_ref[g * rows + comps:(g + 1) * rows, :] = jnp.zeros((rows - comps, LANES), F32)


def steps_body(
    packed_ref, stacked_ref, turned_ref, gains_ref, out_ref, slab_ref, both_ref, turned_a_ref, gain_ref, ghost_ref, again_ref, courant_ref, sems, *, comps
):
    padded = slab_ref.shape[0]
    rows = comps + 6
    groups = padded // rows
    total = groups * comps
    half = both_ref.shape[0] // 2
    loads = ((packed_ref, slab_ref), (gains_ref, gain_ref), (stacked_ref, both_ref), (turned_ref, turned_a_ref))
    copies = [pltpu.make_async_copy(source, target, sems.at[i]) for i, (source, target) in enumerate(loads)]
    for copy in copies:
        copy.start()
    copies[0].wait()
    lane = iota((rows - LANES, LANES), 1)
    columns = jnp.concatenate([slab_ref[(g + 1) * rows - 8:(g + 1) * rows, :] for g in range(groups)] + [jnp.zeros((LANES - 8 * groups, LANES), F32)], axis=0).T
    for g in range(groups):
        start = g * rows
        at = 8 * g + 2
        tail = columns[:, at + 3:at + 4]
        high, low, courant = (jnp.broadcast_to(tail[STEP * i:STEP * (i + 1)], (STEP, LANES)) for i in range(3))
        ghost_ref[start:start + LANES, :] = pltpu.roll(columns, LANES - at - 1, 1)
        ghost_ref[start + LANES:start + rows, :] = jnp.where(lane == 0, low, high)
        courant_ref[start:start + LANES, :] = jnp.broadcast_to(columns[:, at + 2:at + 3], (LANES, LANES))
        courant_ref[start + LANES:start + rows, :] = courant
    blocks = [slice(start, start + BLOCK) for start in range(0, padded, BLOCK)]

    def pairs_and_scale(refs):
        rounded = jnp.concatenate([ref[...].astype(BF16) for ref in refs], axis=1)
        left = jnp.dot(both_ref[0:half, :], rounded, preferred_element_type=F32)
        right = jnp.dot(both_ref[half:2 * half, :], rounded, preferred_element_type=F32)
        squares = jnp.concatenate(
            [sum(jnp.sum(jnp.square(ref[g * rows:g * rows + comps, :]), axis=0, keepdims=True) for g in range(groups)) for ref in refs], axis=1
        )
        spread = jnp.sqrt(squares / total + 1e-06)
        return (left * right).astype(BF16), 1.0 / (1.0 + DISSIPATION * spread)

    for copy in copies[1:]:
        copy.wait()
    pairs, scale = pairs_and_scale((slab_ref, ghost_ref))
    lane = iota((BLOCK, LANES), 1)
    sea = slab_ref[rows - 2:rows - 1, :]
    for block in blocks:
        gain = gain_ref[block, :]
        transfer = jnp.dot(turned_a_ref[block, :], pairs, preferred_element_type=F32)
        field, ghost = (
            (ref[block, :] + gain * ref[block, :] + transfer[:, i * LANES:(i + 1) * LANES]) * scale[:, i * LANES:(i + 1) * LANES]
            for i, ref in enumerate((slab_ref, ghost_ref))
        )
        left = jnp.where(lane == 0, ghost, pltpu.roll(field, 1, 1))
        right = jnp.where(lane == LANES - 1, ghost, pltpu.roll(field, LANES - 1, 1))
        courant = courant_ref[block, :]
        speed = jnp.abs(courant)
        again_ref[block, :] = ((1.0 - speed) * field + speed * jnp.where(courant > 0, left, right)) * sea
    pairs, scale = pairs_and_scale((again_ref,))
    copies = []
    for i, block in enumerate(blocks):
        moved = again_ref[block, :]
        transfer = jnp.dot(turned_a_ref[block, :], pairs, preferred_element_type=F32)
        courant_ref[block, :] = (moved + gain_ref[block, :] * moved + transfer) * scale
        copy = pltpu.make_async_copy(courant_ref.at[block], out_ref.at[block], sems.at[len(loads) + i])
        copy.start()
        copies.append(copy)
    for copy in copies:
        copy.wait()


def gather_body(block_ref, column_ref, slab_ref, offsets_ref, out_ref):
    chunks = slab_ref.shape[0]
    comps = slab_ref.shape[1] - 6
    n = column_ref.shape[0]
    rows = SLAB * n
    slots = NB_BLOCK // n
    block = block_ref[0:1, 0:1]
    device = iota((n, 1), 0)
    start = jnp.sum(jnp.where(device < block, column_ref[...], 0), axis=0, keepdims=True)
    count = jnp.sum(jnp.where(device == block, column_ref[...], 0), axis=0, keepdims=True)
    shift = lax.rem(start, jnp.int32(n))
    lane = iota((1, rows), 1)
    at = lane // SLAB
    slot = lane % SLAB
    wraps = at < shift
    base = jnp.where(wraps, at - shift + n, at - shift)
    line = lax.div(start, jnp.int32(n)) + slot + jnp.where(wraps, 1, 0)
    table = offsets_ref[...]
    wanted = jnp.sum(jnp.where(iota(table.shape, 0) == line, table, 0), axis=0, keepdims=True)
    wanted = jnp.where(jnp.logical_and(slot < slots, base + n * slot < count), wanted, -1)
    point = iota((LANES, rows), 0)
    picked = jnp.zeros((comps, rows), F32)
    for k in range(chunks):
        chosen = (point + k * LANES == wanted).astype(F32).astype(BF16)
        picked = picked + exact_dot(slab_ref[k, 0:comps, :], chosen, ((1,), (0,)))
    side = 2 * LANES
    turned = jnp.concatenate([picked, jnp.zeros((side - comps, rows), F32)], axis=0).T
    out_ref[...] = fold(turned, slots, comps - LANES)


def fold(turned, slots, rest):
    rows = turned.shape[0]
    slot = iota((rows, LANES), 0) % SLAB
    lane = iota((rows, LANES), 1)
    main = turned[:, 0:LANES]
    side = turned[:, LANES:2 * LANES]
    out = jnp.where(slot < slots, main, 0.0)
    for t in range(slots):
        part = pltpu.roll(side, slots - t, 0)
        part = part if t == 0 else pltpu.roll(part, t * rest, 1)
        inside = jnp.logical_and(lane >= t * rest, lane < (t + 1) * rest)
        out = jnp.where(jnp.logical_and(slot == slots, inside), part, out)
    return out


def unfold(value, slots, rest):
    rows = value.shape[0]
    slot = iota((rows, LANES), 0) % SLAB
    lane = iota((rows, LANES), 1)
    side = jnp.zeros((rows, LANES), F32)
    for t in range(slots):
        part = pltpu.roll(value, rows - (slots - t), 0)
        part = part if t == 0 else pltpu.roll(part, LANES - t * rest, 1)
        side = jnp.where(jnp.logical_and(slot == t, lane < rest), part, side)
    return jnp.concatenate([jnp.where(slot < slots, value, 0.0), side], axis=1)


def relay_body(block_ref, column_ref, in_ref, out_ref, *, rest):
    rows = in_ref.shape[0]
    n = rows // SLAB
    slots = NB_BLOCK // n
    me = block_ref[0:1, 0:1]
    wide = jnp.broadcast_to(column_ref[...], (n, rows))
    source = iota((n, rows), 0)
    target = iota((n, rows), 1) // SLAB
    starts = jnp.sum(jnp.where(source < target, wide, 0), axis=0, keepdims=True)
    counts = jnp.sum(jnp.where(source == target, wide, 0), axis=0, keepdims=True)
    span = NB_BLOCK // 2
    slot = iota((1, rows), 1) % SLAB
    position = lax.rem(me - starts + 128 * n, jnp.int32(n)) + n * slot
    valid = jnp.logical_and(position < counts, slot < slots)
    entry = jnp.where(valid, starts + position, -(1 << 20))
    place = iota((rows, 1), 0)
    half = place % SLAB
    place = place // SLAB
    window = jnp.where(place < n // 2, span * place + counts[:, 0:1], span * (place - n // 2)) + n * half
    size = jnp.where(half == 0, n, jnp.where(half == 1, span - n, 0))
    inside = entry - window
    chosen = jnp.logical_and(inside >= 0, inside < size).astype(F32).astype(BF16)
    value = exact_pick(chosen, unfold(in_ref[...], slots, rest))
    out_ref[...] = fold(value, 2, rest)


def settle_body(block_ref, column_ref, in_ref, out_ref):
    comps, span = out_ref.shape
    rows = in_ref.shape[0]
    n = rows // SLAB
    block = block_ref[0:1, 0:1]
    row = iota((rows, LANES), 0)
    device = row // SLAB
    half = row % SLAB
    at = iota((rows, LANES), 1)
    window = jnp.where(block < n // 2, span * block + column_ref[0:1, 0:1], span * (block - n // 2))
    target = lax.rem(device - window + 256 * n, jnp.int32(n)) + n * half
    chosen = jnp.logical_and(at == target, half < 2).astype(F32).astype(BF16)
    value = exact_dot(unfold(in_ref[...], 2, comps - LANES).T, chosen, ((1,), (0,)))
    out_ref[...] = value[0:comps, 0:span]


def per_device(spectrum, courant, growth, quad_a, quad_b, sea_mask, nest_counts, nest_offsets):
    comps, points = spectrum.shape
    total = growth.shape[0]
    groups = lax.axis_size("comp")
    n = lax.axis_size("pts")
    chunks = points // LANES
    padded = 2 * LANES
    packed = jax.ShapeDtypeStruct((chunks, comps + 6, LANES), F32)
    edge = jax.ShapeDtypeStruct((8, padded), F32)
    slab = jax.ShapeDtypeStruct((SLAB * n, LANES), F32)

    side = jnp.concatenate([sea_mask.astype(F32), courant, jnp.zeros((points - comps,), F32)]).reshape(2, points)
    up, down = call(edges_body, (edge, edge), (VMEM, VMEM), (VMEM, VMEM))(spectrum, side)
    before = lax.ppermute(up, "pts", [(i, i + 1) for i in range(n - 1)])
    after = lax.ppermute(down, "pts", [(i + 1, i) for i in range(n - 1)])
    slabs = call(
        pack_body, packed, (VMEM,) * 4, HBM, scratch=(pltpu.VMEM(packed.shape, F32), pltpu.SemaphoreType.DMA((chunks,)))
    )(spectrum, side, before, after)
    slabs = lax.all_to_all(slabs, "comp", split_axis=0, concat_axis=0, tiled=True)

    rows = groups * (comps + 6)
    half = quad_a.shape[0]
    wide = jax.ShapeDtypeStruct((rows, LANES), F32)
    both, turned_a, gain = call(
        functools.partial(stack_body, comps=comps),
        (jax.ShapeDtypeStruct((2 * half, rows), BF16), jax.ShapeDtypeStruct((rows, half), BF16), wide),
        (VMEM, VMEM, VMEM),
        (VMEM, VMEM, VMEM),
        vmem=40,
    )(quad_a.T, quad_b.T, growth.reshape(1, total))
    result = call(
        functools.partial(steps_body, comps=comps),
        wide,
        (HBM, HBM, HBM, HBM),
        HBM,
        scratch=(
            pltpu.VMEM((rows, LANES), F32),
            pltpu.VMEM((2 * half, rows), BF16),
            pltpu.VMEM((rows, half), BF16),
            pltpu.VMEM((rows, LANES), F32),
            pltpu.VMEM((rows, LANES), F32),
            pltpu.VMEM((rows, LANES), F32),
            pltpu.VMEM((rows, LANES), F32),
            pltpu.SemaphoreType.DMA((4 + rows // BLOCK,)),
        ),
        vmem=58,
    )(slabs.reshape(rows, LANES), both, turned_a, gain)
    result = result.reshape(packed.shape)
    result = lax.all_to_all(result, "comp", split_axis=0, concat_axis=0, tiled=True)

    block = jnp.full((1, LANES), lax.axis_index("pts"), jnp.int32)
    column = nest_counts.reshape(n, 1)
    lines = jnp.repeat(jnp.pad(nest_offsets, (0, 4 * n)).reshape(-1, n), SLAB, axis=1)
    sent = call(gather_body, slab, (VMEM,) * 4)(block, column, result, lines)
    sent = lax.all_to_all(sent, "pts", split_axis=0, concat_axis=0, tiled=True)
    field = result[:, 0:comps].transpose(1, 0, 2).reshape(comps, points)
    sent = call(functools.partial(relay_body, rest=comps - LANES), slab, (VMEM,) * 3)(block, column, sent)
    sent = lax.all_to_all(sent, "pts", split_axis=0, concat_axis=0, tiled=True)
    nest = call(settle_body, jax.ShapeDtypeStruct((comps, NB_BLOCK // 2), F32), (VMEM,) * 3)(block, column, sent)
    return (field, nest)


def solution(mesh):
    return jax.shard_map(
        per_device,
        mesh=mesh,
        in_specs=(P("comp", "pts"), P("comp"), P(), P(), P(), P("pts"), P(), P()),
        out_specs=(P("comp", "pts"), P("comp", "pts")),
        check_vma=False,
    )
```

```python
import functools

import jax
import jax.numpy as jnp
from jax import lax
from jax.experimental import pallas as pl
from jax.experimental.pallas import tpu as pltpu
from jax.sharding import PartitionSpec as P

STEPS = 2
LANES = 128
NB_BLOCK = 192
SLAB = 4
BLOCK = 336
DISSIPATION = 0.5

F32 = jnp.float32
BF16 = jnp.bfloat16
VMEM = pl.BlockSpec(memory_space=pltpu.VMEM)
HBM = pl.BlockSpec(memory_space=pltpu.HBM)


def call(body, out_shape, ins, outs=VMEM, scratch=(), vmem=8):
    return pl.pallas_call(
        body,
        out_shape=out_shape,
        in_specs=list(ins),
        out_specs=outs,
        scratch_shapes=list(scratch),
        compiler_params=pltpu.CompilerParams(vmem_limit_bytes=vmem << 20),
        cost_estimate=pl.CostEstimate(flops=1_000_000, bytes_accessed=1_000_000, transcendentals=0),
    )


def iota(shape, axis):
    return lax.broadcasted_iota(jnp.int32, shape, axis)


def split3(value):
    high = value.astype(BF16)
    rest = value - high.astype(F32)
    middle = rest.astype(BF16)
    low = (rest - middle.astype(F32)).astype(BF16)
    return high, middle, low


def exact_dot(value, chosen, dims):
    high, middle, low = (lax.dot_general(term, chosen, (dims, ((), ())), preferred_element_type=F32) for term in split3(value))
    return (high + middle) + low


def exact_pick(chosen, value):
    high, middle, low = (lax.dot_general(chosen, term, (((1,), (0,)), ((), ())), preferred_element_type=F32) for term in split3(value))
    return (high + middle) + low


def edges_body(field_ref, side_ref, up_ref, down_ref):
    comps, points = field_ref.shape
    padded = up_ref.shape[1]
    for ref, start, order in ((up_ref, points - LANES, (LANES - 1, LANES - 2)), (down_ref, 0, (0, 1))):
        tile = jnp.concatenate([field_ref[:, start:start + LANES], jnp.zeros((padded - comps, LANES), F32)], axis=0)
        turned = tile.T
        for row, lane in enumerate(order):
            ref[row:row + 1, :] = turned[lane:lane + 1, :]
        point = start + order[0]
        ref[2:3, :] = jnp.broadcast_to(side_ref[0:1, point:point + 1], (1, padded))
        ref[3:8, :] = jnp.zeros((5, padded), F32)


STEP = 40


def pack_body(field_ref, side_ref, before_ref, after_ref, out_ref, slab_ref, sems):
    comps, points = field_ref.shape
    chunks = points // LANES
    padded = before_ref.shape[1]
    whole = comps // 8 * 8
    rows = jnp.concatenate([before_ref[0:3, :], after_ref[0:3, :], side_ref[1:2, 0:padded], jnp.zeros((1, padded), F32)], axis=0)
    columns = rows.T[:comps, :]

    def wide(at):
        return jnp.broadcast_to(columns[:, at:at + 1], (comps, LANES))

    near_before, far_before, sea_before = wide(0), wide(1), wide(2)
    near_after, far_after, sea_after = wide(3), wide(4), wide(5)
    courant = wide(6)
    speed = jnp.abs(courant)
    stay = 1.0 - speed
    forward = courant > 0
    lane = iota((comps, LANES), 1)

    tiles = [field_ref[:, k * LANES:(k + 1) * LANES] for k in range(chunks)]
    ups = [pltpu.roll(tile, 1, 1) for tile in tiles]
    downs = [pltpu.roll(tile, LANES - 1, 1) for tile in tiles]
    moved = []
    copies = []
    for k in range(chunks):
        left = jnp.where(lane == 0, near_before if k == 0 else ups[k - 1], ups[k])
        right = jnp.where(lane == LANES - 1, near_after if k == chunks - 1 else downs[k + 1], downs[k])
        sea = side_ref[0:1, k * LANES:(k + 1) * LANES]
        value = (stay * tiles[k] + speed * jnp.where(forward, left, right)) * sea
        slab_ref[k, 0:comps, :] = value
        moved.append(value)

    first = jnp.broadcast_to(tiles[0][:, 0:1], (comps, LANES))
    last = jnp.broadcast_to(tiles[chunks - 1][:, LANES - 1:LANES], (comps, LANES))
    moved_before = (stay * near_before + speed * jnp.where(forward, far_before, first)) * sea_before
    moved_after = (stay * near_after + speed * jnp.where(forward, last, far_after)) * sea_after
    ghosts = courant
    for k in range(chunks):
        low = moved_before if k == 0 else pltpu.roll(moved[k - 1], k + 1, 1)
        high = moved_after if k == chunks - 1 else pltpu.roll(moved[k + 1], chunks + k, 1)
        ghosts = jnp.where(lane == k, low, jnp.where(lane == chunks + k, high, ghosts))
    turned = jnp.concatenate([ghosts, jnp.zeros((padded - comps, LANES), F32)], axis=0).T
    head = turned[0:3 * chunks, 0:LANES]
    tail = turned[0:3 * chunks, LANES:2 * LANES]
    mixed = tail[chunks:2 * chunks] + pltpu.roll(tail[0:chunks], STEP, 1) + pltpu.roll(tail[2 * chunks:3 * chunks], 2 * STEP, 1)
    for k in range(chunks):
        slab_ref[k, comps:comps + 1, :] = head[chunks + k:chunks + k + 1]
        slab_ref[k, comps + 1:comps + 2, :] = head[k:k + 1]
        slab_ref[k, comps + 2:comps + 3, :] = head[2 * chunks:2 * chunks + 1]
        slab_ref[k, comps + 3:comps + 4, :] = mixed[k:k + 1]
        slab_ref[k, comps + 4:comps + 5, :] = side_ref[0:1, k * LANES:(k + 1) * LANES]
        slab_ref[k, comps + 5:comps + 6, :] = jnp.zeros((1, LANES), F32)
        copy = pltpu.make_async_copy(slab_ref.at[k], out_ref.at[k], sems.at[k])
        copy.start()
        copies.append(copy)
    for copy in copies:
        copy.wait()


def stack_body(a_ref, b_ref, growth_ref, *refs, comps):
    tables = (len(refs) - 3) // 2
    both_ref, turned_ref, gain_ref = refs[tables:tables + 3]
    for source, target in zip(refs[:tables], refs[tables + 3:]):
        target[...] = source[...]
    total, half = a_ref.shape
    rows = comps + 6
    groups = total // comps
    gap = jnp.zeros((rows - comps, half), F32)
    for at, ref in ((0, a_ref), (half, b_ref)):
        whole = ref[...].astype(F32)
        spread = jnp.concatenate([part for g in range(groups) for part in (whole[g * comps:(g + 1) * comps], gap)], axis=0)
        if at == 0:
            turned_ref[...] = spread.astype(BF16)
        for start in range(0, half, LANES):
            both_ref[at + start:at + start + LANES, :] = spread[:, start:start + LANES].T.astype(BF16)
    growth = growth_ref[...]
    column = jnp.broadcast_to(growth, (8, total)).T[:, 0:1]
    for g in range(groups):
        gain_ref[g * rows:g * rows + comps, :] = jnp.broadcast_to(column[g * comps:(g + 1) * comps], (comps, LANES))
        gain_ref[g * rows + comps:(g + 1) * rows, :] = jnp.zeros((rows - comps, LANES), F32)


def steps_body(
    packed_ref, stacked_ref, turned_ref, gains_ref, out_ref, slab_ref, both_ref, turned_a_ref, gain_ref, ghost_ref, again_ref, courant_ref, sems, *, comps
):
    padded = slab_ref.shape[0]
    rows = comps + 6
    groups = padded // rows
    total = groups * comps
    half = both_ref.shape[0] // 2
    loads = ((packed_ref, slab_ref), (stacked_ref, both_ref), (turned_ref, turned_a_ref), (gains_ref, gain_ref))
    copies = [pltpu.make_async_copy(source, target, sems.at[i]) for i, (source, target) in enumerate(loads)]
    for copy in copies:
        copy.start()
    copies[0].wait()
    lane = iota((rows - LANES, LANES), 1)
    columns = jnp.concatenate([slab_ref[(g + 1) * rows - 8:(g + 1) * rows, :] for g in range(groups)] + [jnp.zeros((LANES - 8 * groups, LANES), F32)], axis=0).T
    for g in range(groups):
        start = g * rows
        at = 8 * g + 2
        tail = columns[:, at + 3:at + 4]
        high, low, courant = (jnp.broadcast_to(tail[STEP * i:STEP * (i + 1)], (STEP, LANES)) for i in range(3))
        ghost_ref[start:start + LANES, :] = pltpu.roll(columns, LANES - at - 1, 1)
        ghost_ref[start + LANES:start + rows, :] = jnp.where(lane == 0, low, high)
        courant_ref[start:start + LANES, :] = jnp.broadcast_to(columns[:, at + 2:at + 3], (LANES, LANES))
        courant_ref[start + LANES:start + rows, :] = courant
    blocks = [slice(start, start + BLOCK) for start in range(0, padded, BLOCK)]

    def pairs_and_scale(refs):
        rounded = jnp.concatenate([ref[...].astype(BF16) for ref in refs], axis=1)
        left = jnp.dot(both_ref[0:half, :], rounded, preferred_element_type=F32)
        right = jnp.dot(both_ref[half:2 * half, :], rounded, preferred_element_type=F32)
        squares = jnp.concatenate(
            [sum(jnp.sum(jnp.square(ref[g * rows:g * rows + comps, :]), axis=0, keepdims=True) for g in range(groups)) for ref in refs], axis=1
        )
        spread = jnp.sqrt(squares / total + 1e-06)
        return (left * right).astype(BF16), 1.0 / (1.0 + DISSIPATION * spread)

    for copy in copies[1:]:
        copy.wait()
    pairs, scale = pairs_and_scale((slab_ref, ghost_ref))
    lane = iota((BLOCK, LANES), 1)
    sea = slab_ref[rows - 2:rows - 1, :]
    for block in blocks:
        gain = gain_ref[block, :]
        transfer = jnp.dot(turned_a_ref[block, :], pairs, preferred_element_type=F32)
        field, ghost = (
            (ref[block, :] + gain * ref[block, :] + transfer[:, i * LANES:(i + 1) * LANES]) * scale[:, i * LANES:(i + 1) * LANES]
            for i, ref in enumerate((slab_ref, ghost_ref))
        )
        left = jnp.where(lane == 0, ghost, pltpu.roll(field, 1, 1))
        right = jnp.where(lane == LANES - 1, ghost, pltpu.roll(field, LANES - 1, 1))
        courant = courant_ref[block, :]
        speed = jnp.abs(courant)
        again_ref[block, :] = ((1.0 - speed) * field + speed * jnp.where(courant > 0, left, right)) * sea
    pairs, scale = pairs_and_scale((again_ref,))
    copies = []
    for i, block in enumerate(blocks):
        moved = again_ref[block, :]
        transfer = jnp.dot(turned_a_ref[block, :], pairs, preferred_element_type=F32)
        courant_ref[block, :] = (moved + gain_ref[block, :] * moved + transfer) * scale
        copy = pltpu.make_async_copy(courant_ref.at[block], out_ref.at[block], sems.at[len(loads) + i])
        copy.start()
        copies.append(copy)
    for copy in copies:
        copy.wait()


def gather_body(block_ref, column_ref, slab_ref, offsets_ref, out_ref):
    chunks = slab_ref.shape[0]
    comps = slab_ref.shape[1] - 6
    n = column_ref.shape[0]
    rows = SLAB * n
    slots = NB_BLOCK // n
    block = block_ref[0:1, 0:1]
    device = iota((n, 1), 0)
    start = jnp.sum(jnp.where(device < block, column_ref[...], 0), axis=0, keepdims=True)
    count = jnp.sum(jnp.where(device == block, column_ref[...], 0), axis=0, keepdims=True)
    shift = lax.rem(start, jnp.int32(n))
    lane = iota((1, rows), 1)
    at = lane // SLAB
    slot = lane % SLAB
    wraps = at < shift
    base = jnp.where(wraps, at - shift + n, at - shift)
    line = lax.div(start, jnp.int32(n)) + slot + jnp.where(wraps, 1, 0)
    table = offsets_ref[...]
    wanted = jnp.sum(jnp.where(iota(table.shape, 0) == line, table, 0), axis=0, keepdims=True)
    wanted = jnp.where(jnp.logical_and(slot < slots, base + n * slot < count), wanted, -1)
    point = iota((LANES, rows), 0)
    picked = jnp.zeros((comps, rows), F32)
    for k in range(chunks):
        chosen = (point + k * LANES == wanted).astype(F32).astype(BF16)
        picked = picked + exact_dot(slab_ref[k, 0:comps, :], chosen, ((1,), (0,)))
    side = 2 * LANES
    turned = jnp.concatenate([picked, jnp.zeros((side - comps, rows), F32)], axis=0).T
    out_ref[...] = fold(turned, slots, comps - LANES)


def fold(turned, slots, rest):
    rows = turned.shape[0]
    slot = iota((rows, LANES), 0) % SLAB
    lane = iota((rows, LANES), 1)
    main = turned[:, 0:LANES]
    side = turned[:, LANES:2 * LANES]
    out = jnp.where(slot < slots, main, 0.0)
    for t in range(slots):
        part = pltpu.roll(side, slots - t, 0)
        part = part if t == 0 else pltpu.roll(part, t * rest, 1)
        inside = jnp.logical_and(lane >= t * rest, lane < (t + 1) * rest)
        out = jnp.where(jnp.logical_and(slot == slots, inside), part, out)
    return out


def unfold(value, slots, rest):
    rows = value.shape[0]
    slot = iota((rows, LANES), 0) % SLAB
    lane = iota((rows, LANES), 1)
    side = jnp.zeros((rows, LANES), F32)
    for t in range(slots):
        part = pltpu.roll(value, rows - (slots - t), 0)
        part = part if t == 0 else pltpu.roll(part, LANES - t * rest, 1)
        side = jnp.where(jnp.logical_and(slot == t, lane < rest), part, side)
    return jnp.concatenate([jnp.where(slot < slots, value, 0.0), side], axis=1)


def relay_body(block_ref, column_ref, in_ref, out_ref, *, rest):
    rows = in_ref.shape[0]
    n = rows // SLAB
    slots = NB_BLOCK // n
    me = block_ref[0:1, 0:1]
    wide = jnp.broadcast_to(column_ref[...], (n, rows))
    source = iota((n, rows), 0)
    target = iota((n, rows), 1) // SLAB
    starts = jnp.sum(jnp.where(source < target, wide, 0), axis=0, keepdims=True)
    counts = jnp.sum(jnp.where(source == target, wide, 0), axis=0, keepdims=True)
    span = NB_BLOCK // 2
    slot = iota((1, rows), 1) % SLAB
    position = lax.rem(me - starts + 128 * n, jnp.int32(n)) + n * slot
    valid = jnp.logical_and(position < counts, slot < slots)
    entry = jnp.where(valid, starts + position, -(1 << 20))
    place = iota((rows, 1), 0)
    half = place % SLAB
    place = place // SLAB
    window = jnp.where(place < n // 2, span * place + counts[:, 0:1], span * (place - n // 2)) + n * half
    size = jnp.where(half == 0, n, jnp.where(half == 1, span - n, 0))
    inside = entry - window
    chosen = jnp.logical_and(inside >= 0, inside < size).astype(F32).astype(BF16)
    value = exact_pick(chosen, unfold(in_ref[...], slots, rest))
    out_ref[...] = fold(value, 2, rest)


def settle_body(block_ref, column_ref, in_ref, out_ref):
    comps, span = out_ref.shape
    rows = in_ref.shape[0]
    n = rows // SLAB
    block = block_ref[0:1, 0:1]
    row = iota((rows, LANES), 0)
    device = row // SLAB
    half = row % SLAB
    at = iota((rows, LANES), 1)
    window = jnp.where(block < n // 2, span * block + column_ref[0:1, 0:1], span * (block - n // 2))
    target = lax.rem(device - window + 256 * n, jnp.int32(n)) + n * half
    chosen = jnp.logical_and(at == target, half < 2).astype(F32).astype(BF16)
    value = exact_dot(unfold(in_ref[...], 2, comps - LANES).T, chosen, ((1,), (0,)))
    out_ref[...] = value[0:comps, 0:span]


def per_device(spectrum, courant, growth, quad_a, quad_b, sea_mask, nest_counts, nest_offsets):
    comps, points = spectrum.shape
    total = growth.shape[0]
    groups = lax.axis_size("comp")
    n = lax.axis_size("pts")
    chunks = points // LANES
    padded = 2 * LANES
    packed = jax.ShapeDtypeStruct((chunks, comps + 6, LANES), F32)
    edge = jax.ShapeDtypeStruct((8, padded), F32)
    slab = jax.ShapeDtypeStruct((SLAB * n, LANES), F32)

    zero = jnp.zeros((), F32)
    side = lax.pad(sea_mask.astype(F32), zero, ((0, points, 0),)) + lax.pad(courant, zero, ((points, points - comps, 0),))
    side = side.reshape(2, points)
    up, down = call(edges_body, (edge, edge), (VMEM, VMEM), (VMEM, VMEM))(spectrum, side)
    before = lax.ppermute(up, "pts", [(i, i + 1) for i in range(n - 1)])
    after = lax.ppermute(down, "pts", [(i + 1, i) for i in range(n - 1)])
    slabs = call(
        pack_body, packed, (VMEM,) * 4, HBM, scratch=(pltpu.VMEM(packed.shape, F32), pltpu.SemaphoreType.DMA((chunks,)))
    )(spectrum, side, before, after)
    slabs = lax.all_to_all(slabs, "comp", split_axis=0, concat_axis=0, tiled=True)

    block = jnp.full((1, LANES), lax.axis_index("pts"), jnp.int32)
    column = nest_counts.reshape(n, 1)
    lines = jnp.repeat(jnp.pad(nest_offsets, (0, 4 * n)).reshape(-1, n), SLAB, axis=1)
    rows = groups * (comps + 6)
    half = quad_a.shape[0]
    wide = jax.ShapeDtypeStruct((rows, LANES), F32)
    tables = (block, column, lines)
    both, turned_a, gain, block, column, lines = call(
        functools.partial(stack_body, comps=comps),
        (jax.ShapeDtypeStruct((2 * half, rows), BF16), jax.ShapeDtypeStruct((rows, half), BF16), wide)
        + tuple(jax.ShapeDtypeStruct(table.shape, table.dtype) for table in tables),
        (VMEM,) * 6,
        (VMEM,) * 6,
        vmem=40,
    )(quad_a.T, quad_b.T, growth.reshape(1, total), *tables)
    result = call(
        functools.partial(steps_body, comps=comps),
        wide,
        (HBM, HBM, HBM, HBM),
        HBM,
        scratch=(
            pltpu.VMEM((rows, LANES), F32),
            pltpu.VMEM((2 * half, rows), BF16),
            pltpu.VMEM((rows, half), BF16),
            pltpu.VMEM((rows, LANES), F32),
            pltpu.VMEM((rows, LANES), F32),
            pltpu.VMEM((rows, LANES), F32),
            pltpu.VMEM((rows, LANES), F32),
            pltpu.SemaphoreType.DMA((4 + rows // BLOCK,)),
        ),
        vmem=58,
    )(slabs.reshape(rows, LANES), both, turned_a, gain)
    result = result.reshape(packed.shape)
    result = lax.all_to_all(result, "comp", split_axis=0, concat_axis=0, tiled=True)

    sent = call(gather_body, slab, (VMEM,) * 4)(block, column, result, lines)
    sent = lax.all_to_all(sent, "pts", split_axis=0, concat_axis=0, tiled=True)
    field = result[:, 0:comps].transpose(1, 0, 2).reshape(comps, points)
    sent = call(functools.partial(relay_body, rest=comps - LANES), slab, (VMEM,) * 3)(block, column, sent)
    sent = lax.all_to_all(sent, "pts", split_axis=0, concat_axis=0, tiled=True)
    nest = call(settle_body, jax.ShapeDtypeStruct((comps, NB_BLOCK // 2), F32), (VMEM,) * 3)(block, column, sent)
    return (field, nest)


def solution(mesh):
    return jax.shard_map(
        per_device,
        mesh=mesh,
        in_specs=(P("comp", "pts"), P("comp"), P(), P(), P(), P("pts"), P(), P()),
        out_specs=(P("comp", "pts"), P("comp", "pts")),
        check_vma=False,
    )
```

```python
import functools

import jax
import jax.numpy as jnp
from jax import lax
from jax.experimental import pallas as pl
from jax.experimental.pallas import tpu as pltpu
from jax.sharding import PartitionSpec as P

STEPS = 2
LANES = 128
NB_BLOCK = 192
SLAB = 4
BLOCK = 336
DISSIPATION = 0.5

F32 = jnp.float32
BF16 = jnp.bfloat16
VMEM = pl.BlockSpec(memory_space=pltpu.VMEM)
HBM = pl.BlockSpec(memory_space=pltpu.HBM)


def call(body, out_shape, ins, outs=VMEM, scratch=(), vmem=8):
    return pl.pallas_call(
        body,
        out_shape=out_shape,
        in_specs=list(ins),
        out_specs=outs,
        scratch_shapes=list(scratch),
        compiler_params=pltpu.CompilerParams(vmem_limit_bytes=vmem << 20),
        cost_estimate=pl.CostEstimate(flops=1_000_000, bytes_accessed=1_000_000, transcendentals=0),
    )


def iota(shape, axis):
    return lax.broadcasted_iota(jnp.int32, shape, axis)


def split3(value):
    high = value.astype(BF16)
    rest = value - high.astype(F32)
    middle = rest.astype(BF16)
    low = (rest - middle.astype(F32)).astype(BF16)
    return high, middle, low


def exact_dot(value, chosen, dims):
    high, middle, low = (lax.dot_general(term, chosen, (dims, ((), ())), preferred_element_type=F32) for term in split3(value))
    return (high + middle) + low


def exact_pick(chosen, value):
    high, middle, low = (lax.dot_general(chosen, term, (((1,), (0,)), ((), ())), preferred_element_type=F32) for term in split3(value))
    return (high + middle) + low


def edges_body(field_ref, side_ref, up_ref, down_ref):
    comps, points = field_ref.shape
    padded = up_ref.shape[1]
    for ref, start, order in ((up_ref, points - LANES, (LANES - 1, LANES - 2)), (down_ref, 0, (0, 1))):
        tile = jnp.concatenate([field_ref[:, start:start + LANES], jnp.zeros((padded - comps, LANES), F32)], axis=0)
        turned = tile.T
        for row, lane in enumerate(order):
            ref[row:row + 1, :] = turned[lane:lane + 1, :]
        point = start + order[0]
        ref[2:3, :] = jnp.broadcast_to(side_ref[0:1, point:point + 1], (1, padded))
        ref[3:8, :] = jnp.zeros((5, padded), F32)


STEP = 40


def pack_body(field_ref, side_ref, before_ref, after_ref, out_ref, slab_ref, sems):
    comps, points = field_ref.shape
    chunks = points // LANES
    padded = before_ref.shape[1]
    whole = comps // 8 * 8
    rows = jnp.concatenate([before_ref[0:3, :], after_ref[0:3, :], side_ref[1:2, 0:padded], jnp.zeros((1, padded), F32)], axis=0)
    columns = rows.T[:comps, :]

    def wide(at):
        return jnp.broadcast_to(columns[:, at:at + 1], (comps, LANES))

    near_before, far_before, sea_before = wide(0), wide(1), wide(2)
    near_after, far_after, sea_after = wide(3), wide(4), wide(5)
    courant = wide(6)
    speed = jnp.abs(courant)
    stay = 1.0 - speed
    forward = courant > 0
    lane = iota((comps, LANES), 1)

    tiles = [field_ref[:, k * LANES:(k + 1) * LANES] for k in range(chunks)]
    ups = [pltpu.roll(tile, 1, 1) for tile in tiles]
    downs = [pltpu.roll(tile, LANES - 1, 1) for tile in tiles]
    moved = []
    copies = []
    for k in range(chunks):
        left = jnp.where(lane == 0, near_before if k == 0 else ups[k - 1], ups[k])
        right = jnp.where(lane == LANES - 1, near_after if k == chunks - 1 else downs[k + 1], downs[k])
        sea = side_ref[0:1, k * LANES:(k + 1) * LANES]
        value = (stay * tiles[k] + speed * jnp.where(forward, left, right)) * sea
        slab_ref[k, 0:comps, :] = value
        moved.append(value)

    first = jnp.broadcast_to(tiles[0][:, 0:1], (comps, LANES))
    last = jnp.broadcast_to(tiles[chunks - 1][:, LANES - 1:LANES], (comps, LANES))
    moved_before = (stay * near_before + speed * jnp.where(forward, far_before, first)) * sea_before
    moved_after = (stay * near_after + speed * jnp.where(forward, last, far_after)) * sea_after
    ghosts = courant
    for k in range(chunks):
        low = moved_before if k == 0 else pltpu.roll(moved[k - 1], k + 1, 1)
        high = moved_after if k == chunks - 1 else pltpu.roll(moved[k + 1], chunks + k, 1)
        ghosts = jnp.where(lane == k, low, jnp.where(lane == chunks + k, high, ghosts))
    turned = jnp.concatenate([ghosts, jnp.zeros((padded - comps, LANES), F32)], axis=0).T
    head = turned[0:3 * chunks, 0:LANES]
    tail = turned[0:3 * chunks, LANES:2 * LANES]
    mixed = tail[chunks:2 * chunks] + pltpu.roll(tail[0:chunks], STEP, 1) + pltpu.roll(tail[2 * chunks:3 * chunks], 2 * STEP, 1)
    for k in range(chunks):
        slab_ref[k, comps:comps + 1, :] = head[chunks + k:chunks + k + 1]
        slab_ref[k, comps + 1:comps + 2, :] = head[k:k + 1]
        slab_ref[k, comps + 2:comps + 3, :] = head[2 * chunks:2 * chunks + 1]
        slab_ref[k, comps + 3:comps + 4, :] = mixed[k:k + 1]
        slab_ref[k, comps + 4:comps + 5, :] = side_ref[0:1, k * LANES:(k + 1) * LANES]
        slab_ref[k, comps + 5:comps + 6, :] = jnp.zeros((1, LANES), F32)
        copy = pltpu.make_async_copy(slab_ref.at[k], out_ref.at[k], sems.at[k])
        copy.start()
        copies.append(copy)
    for copy in copies:
        copy.wait()


def stack_body(a_ref, b_ref, growth_ref, both_ref, turned_ref, gain_ref, *, comps):
    total, half = a_ref.shape
    rows = comps + 6
    groups = total // comps
    gap = jnp.zeros((rows - comps, half), F32)
    for at, ref in ((0, a_ref), (half, b_ref)):
        whole = ref[...].astype(F32)
        spread = jnp.concatenate([part for g in range(groups) for part in (whole[g * comps:(g + 1) * comps], gap)], axis=0)
        if at == 0:
            turned_ref[...] = spread.astype(BF16)
        for start in range(0, half, LANES):
            both_ref[at + start:at + start + LANES, :] = spread[:, start:start + LANES].T.astype(BF16)
    growth = growth_ref[...]
    column = jnp.broadcast_to(growth, (8, total)).T[:, 0:1]
    for g in range(groups):
        gain_ref[g * rows:g * rows + comps, :] = jnp.broadcast_to(column[g * comps:(g + 1) * comps], (comps, LANES))
        gain_ref[g * rows + comps:(g + 1) * rows, :] = jnp.zeros((rows - comps, LANES), F32)


def steps_body(
    packed_ref, stacked_ref, turned_ref, gains_ref, out_ref, slab_ref, both_ref, turned_a_ref, gain_ref, ghost_ref, again_ref, courant_ref, sems, *, comps
):
    padded = slab_ref.shape[0]
    rows = comps + 6
    groups = padded // rows
    total = groups * comps
    half = both_ref.shape[0] // 2
    loads = ((packed_ref, slab_ref), (stacked_ref, both_ref), (turned_ref, turned_a_ref), (gains_ref, gain_ref))
    copies = [pltpu.make_async_copy(source, target, sems.at[i]) for i, (source, target) in enumerate(loads)]
    for copy in copies:
        copy.start()
    copies[0].wait()
    lane = iota((rows - LANES, LANES), 1)
    columns = jnp.concatenate([slab_ref[(g + 1) * rows - 8:(g + 1) * rows, :] for g in range(groups)] + [jnp.zeros((LANES - 8 * groups, LANES), F32)], axis=0).T
    for g in range(groups):
        start = g * rows
        at = 8 * g + 2
        tail = columns[:, at + 3:at + 4]
        high, low, courant = (jnp.broadcast_to(tail[STEP * i:STEP * (i + 1)], (STEP, LANES)) for i in range(3))
        ghost_ref[start:start + LANES, :] = pltpu.roll(columns, LANES - at - 1, 1)
        ghost_ref[start + LANES:start + rows, :] = jnp.where(lane == 0, low, high)
        courant_ref[start:start + LANES, :] = jnp.broadcast_to(columns[:, at + 2:at + 3], (LANES, LANES))
        courant_ref[start + LANES:start + rows, :] = courant
    blocks = [slice(start, start + BLOCK) for start in range(0, padded, BLOCK)]

    def pairs_and_scale(refs):
        rounded = jnp.concatenate([ref[...].astype(BF16) for ref in refs], axis=1)
        left = jnp.dot(both_ref[0:half, :], rounded, preferred_element_type=F32)
        right = jnp.dot(both_ref[half:2 * half, :], rounded, preferred_element_type=F32)
        squares = jnp.concatenate(
            [sum(jnp.sum(jnp.square(ref[g * rows:g * rows + comps, :]), axis=0, keepdims=True) for g in range(groups)) for ref in refs], axis=1
        )
        spread = jnp.sqrt(squares / total + 1e-06)
        return (left * right).astype(BF16), 1.0 / (1.0 + DISSIPATION * spread)

    for copy in copies[1:]:
        copy.wait()
    pairs, scale = pairs_and_scale((slab_ref, ghost_ref))
    lane = iota((BLOCK, LANES), 1)
    sea = slab_ref[rows - 2:rows - 1, :]
    for block in blocks:
        gain = gain_ref[block, :]
        transfer = jnp.dot(turned_a_ref[block, :], pairs, preferred_element_type=F32)
        field, ghost = (
            (ref[block, :] + gain * ref[block, :] + transfer[:, i * LANES:(i + 1) * LANES]) * scale[:, i * LANES:(i + 1) * LANES]
            for i, ref in enumerate((slab_ref, ghost_ref))
        )
        left = jnp.where(lane == 0, ghost, pltpu.roll(field, 1, 1))
        right = jnp.where(lane == LANES - 1, ghost, pltpu.roll(field, LANES - 1, 1))
        courant = courant_ref[block, :]
        speed = jnp.abs(courant)
        again_ref[block, :] = ((1.0 - speed) * field + speed * jnp.where(courant > 0, left, right)) * sea
    pairs, scale = pairs_and_scale((again_ref,))
    copies = []
    for i, block in enumerate(blocks):
        moved = again_ref[block, :]
        transfer = jnp.dot(turned_a_ref[block, :], pairs, preferred_element_type=F32)
        courant_ref[block, :] = (moved + gain_ref[block, :] * moved + transfer) * scale
        copy = pltpu.make_async_copy(courant_ref.at[block], out_ref.at[block], sems.at[len(loads) + i])
        copy.start()
        copies.append(copy)
    for copy in copies:
        copy.wait()


def plan_body(block_ref, column_ref, offsets_ref, pick_ref, relay_ref, place_ref):
    n = column_ref.shape[0]
    rows = SLAB * n
    slots = NB_BLOCK // n
    span = NB_BLOCK // 2
    block = block_ref[0:1, 0:1]
    column = column_ref[...]

    def ones(mask):
        return mask.astype(F32).astype(BF16)

    device = iota((n, 1), 0)
    start = jnp.sum(jnp.where(device < block, column, 0), axis=0, keepdims=True)
    count = jnp.sum(jnp.where(device == block, column, 0), axis=0, keepdims=True)
    shift = lax.rem(start, jnp.int32(n))
    lane = iota((1, rows), 1)
    at = lane // SLAB
    slot = lane % SLAB
    wraps = at < shift
    base = jnp.where(wraps, at - shift + n, at - shift)
    line = lax.div(start, jnp.int32(n)) + slot + jnp.where(wraps, 1, 0)
    table = offsets_ref[...]
    wanted = jnp.sum(jnp.where(iota(table.shape, 0) == line, table, 0), axis=0, keepdims=True)
    wanted = jnp.where(jnp.logical_and(slot < slots, base + n * slot < count), wanted, -1)
    pick_ref[...] = ones(iota(pick_ref.shape, 0) == wanted)

    wide = jnp.broadcast_to(column, (n, rows))
    source = iota((n, rows), 0)
    target = iota((n, rows), 1) // SLAB
    starts = jnp.sum(jnp.where(source < target, wide, 0), axis=0, keepdims=True)
    counts = jnp.sum(jnp.where(source == target, wide, 0), axis=0, keepdims=True)
    position = lax.rem(block - starts + 128 * n, jnp.int32(n)) + n * slot
    entry = jnp.where(jnp.logical_and(position < counts, slot < slots), starts + position, -(1 << 20))
    row = iota((rows, 1), 0)
    half = row % SLAB
    place = row // SLAB
    window = jnp.where(place < n // 2, span * place + counts[:, 0:1], span * (place - n // 2)) + n * half
    size = jnp.where(half == 0, n, jnp.where(half == 1, span - n, 0))
    inside = entry - window
    relay_ref[...] = ones(jnp.logical_and(inside >= 0, inside < size))

    own = jnp.where(block < n // 2, span * block + column[0:1, 0:1], span * (block - n // 2))
    goal = lax.rem(place - own + 256 * n, jnp.int32(n)) + n * half
    place_ref[...] = ones(jnp.logical_and(iota((rows, LANES), 1) == goal, half < 2))


def gather_body(pick_ref, slab_ref, out_ref, *, slots):
    chunks = slab_ref.shape[0]
    comps = slab_ref.shape[1] - 6
    rows = pick_ref.shape[1]
    picked = jnp.zeros((comps, rows), F32)
    for k in range(chunks):
        picked = picked + exact_dot(slab_ref[k, 0:comps, :], pick_ref[k * LANES:(k + 1) * LANES, :], ((1,), (0,)))
    side = 2 * LANES
    turned = jnp.concatenate([picked, jnp.zeros((side - comps, rows), F32)], axis=0).T
    out_ref[...] = fold(turned, slots, comps - LANES)


def fold(turned, slots, rest):
    rows = turned.shape[0]
    slot = iota((rows, LANES), 0) % SLAB
    lane = iota((rows, LANES), 1)
    main = turned[:, 0:LANES]
    side = turned[:, LANES:2 * LANES]
    out = jnp.where(slot < slots, main, 0.0)
    for t in range(slots):
        part = pltpu.roll(side, slots - t, 0)
        part = part if t == 0 else pltpu.roll(part, t * rest, 1)
        inside = jnp.logical_and(lane >= t * rest, lane < (t + 1) * rest)
        out = jnp.where(jnp.logical_and(slot == slots, inside), part, out)
    return out


def unfold(value, slots, rest):
    rows = value.shape[0]
    slot = iota((rows, LANES), 0) % SLAB
    lane = iota((rows, LANES), 1)
    side = jnp.zeros((rows, LANES), F32)
    for t in range(slots):
        part = pltpu.roll(value, rows - (slots - t), 0)
        part = part if t == 0 else pltpu.roll(part, LANES - t * rest, 1)
        side = jnp.where(jnp.logical_and(slot == t, lane < rest), part, side)
    return jnp.concatenate([jnp.where(slot < slots, value, 0.0), side], axis=1)


def relay_body(chosen_ref, in_ref, out_ref, *, slots, rest):
    out_ref[...] = fold(exact_pick(chosen_ref[...], unfold(in_ref[...], slots, rest)), 2, rest)


def settle_body(chosen_ref, in_ref, out_ref):
    comps, span = out_ref.shape
    value = exact_dot(unfold(in_ref[...], 2, comps - LANES).T, chosen_ref[...], ((1,), (0,)))
    out_ref[...] = value[0:comps, 0:span]


def per_device(spectrum, courant, growth, quad_a, quad_b, sea_mask, nest_counts, nest_offsets):
    comps, points = spectrum.shape
    total = growth.shape[0]
    groups = lax.axis_size("comp")
    n = lax.axis_size("pts")
    chunks = points // LANES
    padded = 2 * LANES
    packed = jax.ShapeDtypeStruct((chunks, comps + 6, LANES), F32)
    edge = jax.ShapeDtypeStruct((8, padded), F32)
    slab = jax.ShapeDtypeStruct((SLAB * n, LANES), F32)

    zero = jnp.zeros((), F32)
    side = lax.pad(sea_mask, jnp.int32(0), ((0, points, 0),)).astype(F32) + lax.pad(courant, zero, ((points, points - comps, 0),))
    side = side.reshape(2, points)
    up, down = call(edges_body, (edge, edge), (VMEM, VMEM), (VMEM, VMEM))(spectrum, side)
    before = lax.ppermute(up, "pts", [(i, i + 1) for i in range(n - 1)])
    after = lax.ppermute(down, "pts", [(i + 1, i) for i in range(n - 1)])
    slabs = call(
        pack_body, packed, (VMEM,) * 4, HBM, scratch=(pltpu.VMEM(packed.shape, F32), pltpu.SemaphoreType.DMA((chunks,)))
    )(spectrum, side, before, after)
    slabs = lax.all_to_all(slabs, "comp", split_axis=0, concat_axis=0, tiled=True)

    block = jnp.full((1, LANES), lax.axis_index("pts"), jnp.int32)
    column = nest_counts.reshape(n, 1)
    lines = jnp.repeat(jnp.pad(nest_offsets, (0, 4 * n)).reshape(-1, n), SLAB, axis=1)
    pick, relay, place = call(
        plan_body,
        tuple(jax.ShapeDtypeStruct(shape, BF16) for shape in ((points, SLAB * n), (SLAB * n, SLAB * n), (SLAB * n, LANES))),
        (VMEM,) * 3,
        (VMEM,) * 3,
    )(block, column, lines)
    rows = groups * (comps + 6)
    half = quad_a.shape[0]
    wide = jax.ShapeDtypeStruct((rows, LANES), F32)
    both, turned_a, gain = call(
        functools.partial(stack_body, comps=comps),
        (jax.ShapeDtypeStruct((2 * half, rows), BF16), jax.ShapeDtypeStruct((rows, half), BF16), wide),
        (VMEM,) * 3,
        (VMEM,) * 3,
        vmem=40,
    )(quad_a.T, quad_b.T, growth.reshape(1, total))
    result = call(
        functools.partial(steps_body, comps=comps),
        wide,
        (HBM, HBM, HBM, HBM),
        HBM,
        scratch=(
            pltpu.VMEM((rows, LANES), F32),
            pltpu.VMEM((2 * half, rows), BF16),
            pltpu.VMEM((rows, half), BF16),
            pltpu.VMEM((rows, LANES), F32),
            pltpu.VMEM((rows, LANES), F32),
            pltpu.VMEM((rows, LANES), F32),
            pltpu.VMEM((rows, LANES), F32),
            pltpu.SemaphoreType.DMA((4 + rows // BLOCK,)),
        ),
        vmem=58,
    )(slabs.reshape(rows, LANES), both, turned_a, gain)
    result = result.reshape(packed.shape)
    result = lax.all_to_all(result, "comp", split_axis=0, concat_axis=0, tiled=True)

    slots = NB_BLOCK // n
    sent = call(functools.partial(gather_body, slots=slots), slab, (VMEM,) * 2)(pick, result)
    sent = lax.all_to_all(sent, "pts", split_axis=0, concat_axis=0, tiled=True)
    field = result[:, 0:comps].transpose(1, 0, 2).reshape(comps, points)
    sent = call(functools.partial(relay_body, slots=slots, rest=comps - LANES), slab, (VMEM,) * 2)(relay, sent)
    sent = lax.all_to_all(sent, "pts", split_axis=0, concat_axis=0, tiled=True)
    nest = call(settle_body, jax.ShapeDtypeStruct((comps, NB_BLOCK // 2), F32), (VMEM,) * 2)(place, sent)
    return (field, nest)


def solution(mesh):
    return jax.shard_map(
        per_device,
        mesh=mesh,
        in_specs=(P("comp", "pts"), P("comp"), P(), P(), P(), P("pts"), P(), P()),
        out_specs=(P("comp", "pts"), P("comp", "pts")),
        check_vma=False,
    )
```

```python
import functools

import jax
import jax.numpy as jnp
from jax import lax
from jax.experimental import pallas as pl
from jax.experimental.pallas import tpu as pltpu
from jax.sharding import PartitionSpec as P

STEPS = 2
LANES = 128
NB_BLOCK = 192
SLAB = 4
BLOCK = 336
DISSIPATION = 0.5

F32 = jnp.float32
BF16 = jnp.bfloat16
VMEM = pl.BlockSpec(memory_space=pltpu.VMEM)
HBM = pl.BlockSpec(memory_space=pltpu.HBM)


def call(body, out_shape, ins, outs=VMEM, scratch=(), vmem=8):
    return pl.pallas_call(
        body,
        out_shape=out_shape,
        in_specs=list(ins),
        out_specs=outs,
        scratch_shapes=list(scratch),
        compiler_params=pltpu.CompilerParams(vmem_limit_bytes=vmem << 20),
        cost_estimate=pl.CostEstimate(flops=1_000_000, bytes_accessed=1_000_000, transcendentals=0),
    )


def iota(shape, axis):
    return lax.broadcasted_iota(jnp.int32, shape, axis)


def split3(value):
    high = value.astype(BF16)
    rest = value - high.astype(F32)
    middle = rest.astype(BF16)
    low = (rest - middle.astype(F32)).astype(BF16)
    return high, middle, low


def exact_dot(value, chosen, dims):
    high, middle, low = (lax.dot_general(term, chosen, (dims, ((), ())), preferred_element_type=F32) for term in split3(value))
    return (high + middle) + low


def exact_pick(chosen, value):
    high, middle, low = (lax.dot_general(chosen, term, (((1,), (0,)), ((), ())), preferred_element_type=F32) for term in split3(value))
    return (high + middle) + low


def edges_body(block_ref, field_ref, side_ref, pair_ref, next_ref):
    comps, points = field_ref.shape
    padded = pair_ref.shape[1]
    payloads = []
    for start, order in ((points - LANES, (LANES - 1, LANES - 2)), (0, (0, 1))):
        tile = jnp.concatenate([field_ref[:, start:start + LANES], jnp.zeros((padded - comps, LANES), F32)], axis=0)
        turned = tile.T
        point = start + order[0]
        sea = jnp.broadcast_to(side_ref[0:1, point:point + 1], (1, padded))
        payloads.append(jnp.concatenate([turned[lane:lane + 1, :] for lane in order] + [sea, jnp.zeros((5, padded), F32)], axis=0))
    up, down = payloads
    even = lax.rem(block_ref[0:1, 0:1], jnp.int32(2)) == 0
    pair_ref[...] = jnp.where(even, up, down)
    next_ref[...] = jnp.where(even, down, up)


STEP = 40


def rows_of(chosen, value):
    high, middle, low = (lax.dot_general(chosen, term, (((1,), (1,)), ((), ())), preferred_element_type=F32) for term in split3(value))
    return (high + middle) + low


def pack_body(block_ref, field_ref, side_ref, pair_ref, next_ref, out_ref, slab_ref, sems):
    comps, points = field_ref.shape
    chunks = points // LANES
    padded = pair_ref.shape[1]
    even = lax.rem(block_ref[0:1, 0:1], jnp.int32(2)) == 0
    before = jnp.where(even, next_ref[...], pair_ref[...])
    after = jnp.where(even, pair_ref[...], next_ref[...])
    courant_row = side_ref[1:2, 0:padded]
    columns = jnp.concatenate([before[0:1], after[0:1], courant_row, jnp.zeros((5, padded), F32)], axis=0).T[:comps, :]

    def wide(at):
        return jnp.broadcast_to(columns[:, at:at + 1], (comps, LANES))

    near_before, near_after, courant = wide(0), wide(1), wide(2)
    speed = jnp.abs(courant)
    stay = 1.0 - speed
    forward = courant > 0
    lane = iota((comps, LANES), 1)

    tiles = [field_ref[:, k * LANES:(k + 1) * LANES] for k in range(chunks)]
    ups = [pltpu.roll(tile, 1, 1) for tile in tiles]
    downs = [pltpu.roll(tile, LANES - 1, 1) for tile in tiles]
    moved = []
    copies = []
    for k in range(chunks):
        left = jnp.where(lane == 0, near_before if k == 0 else ups[k - 1], ups[k])
        right = jnp.where(lane == LANES - 1, near_after if k == chunks - 1 else downs[k + 1], downs[k])
        sea = side_ref[0:1, k * LANES:(k + 1) * LANES]
        value = (stay * tiles[k] + speed * jnp.where(forward, left, right)) * sea
        slab_ref[k, 0:comps, :] = value
        moved.append(value)

    count = 2 * chunks
    row = iota((count, LANES), 0)
    at = iota((count, LANES), 1)

    def picked(value, last_to, first_to):
        mask = jnp.logical_or(jnp.logical_and(at == LANES - 1, row == last_to), jnp.logical_and(at == 0, row == first_to))
        return rows_of(mask.astype(F32).astype(BF16), value)

    ghosts = sum(picked(moved[k], k + 1 if k < chunks - 1 else -1, chunks + k - 1 if k > 0 else -1) for k in range(chunks))
    outer = picked(tiles[0], -1, 0) + picked(tiles[chunks - 1], 1, -1)
    gap = jnp.zeros((count, padded - comps), F32)
    ghosts, outer = (jnp.concatenate([value, gap], axis=1) for value in (ghosts, outer))
    speed_row = jnp.abs(courant_row)
    stay_row = 1.0 - speed_row
    forward_row = courant_row > 0
    moved_before = (stay_row * before[0:1] + speed_row * jnp.where(forward_row, before[1:2], outer[0:1])) * before[2:3]
    moved_after = (stay_row * after[0:1] + speed_row * jnp.where(forward_row, outer[1:2], after[1:2])) * after[2:3]
    row = iota((count, padded), 0)
    ghosts = jnp.where(row == 0, moved_before, jnp.where(row == count - 1, moved_after, ghosts))
    head = ghosts[:, 0:LANES]
    tail = ghosts[:, LANES:2 * LANES]
    mixed = tail[chunks:count] + pltpu.roll(tail[0:chunks], STEP, 1) + pltpu.roll(courant_row[:, LANES:2 * LANES], 2 * STEP, 1)
    for k in range(chunks):
        slab_ref[k, comps:comps + 1, :] = head[chunks + k:chunks + k + 1]
        slab_ref[k, comps + 1:comps + 2, :] = head[k:k + 1]
        slab_ref[k, comps + 2:comps + 3, :] = courant_row[:, 0:LANES]
        slab_ref[k, comps + 3:comps + 4, :] = mixed[k:k + 1]
        slab_ref[k, comps + 4:comps + 5, :] = side_ref[0:1, k * LANES:(k + 1) * LANES]
        slab_ref[k, comps + 5:comps + 6, :] = jnp.zeros((1, LANES), F32)
        copy = pltpu.make_async_copy(slab_ref.at[k], out_ref.at[k], sems.at[k])
        copy.start()
        copies.append(copy)
    for copy in copies:
        copy.wait()


def stack_body(a_ref, b_ref, growth_ref, both_ref, turned_ref, gain_ref, *, comps):
    total, half = a_ref.shape
    rows = comps + 6
    groups = total // comps
    gap = jnp.zeros((rows - comps, half), F32)
    for at, ref in ((0, a_ref), (half, b_ref)):
        whole = ref[...].astype(F32)
        spread = jnp.concatenate([part for g in range(groups) for part in (whole[g * comps:(g + 1) * comps], gap)], axis=0)
        if at == 0:
            turned_ref[...] = spread.astype(BF16)
        for start in range(0, half, LANES):
            both_ref[at + start:at + start + LANES, :] = spread[:, start:start + LANES].T.astype(BF16)
    growth = growth_ref[...]
    column = jnp.broadcast_to(growth, (8, total)).T[:, 0:1]
    for g in range(groups):
        gain_ref[g * rows:g * rows + comps, :] = jnp.broadcast_to(column[g * comps:(g + 1) * comps], (comps, LANES))
        gain_ref[g * rows + comps:(g + 1) * rows, :] = jnp.zeros((rows - comps, LANES), F32)


def steps_body(
    packed_ref, stacked_ref, turned_ref, gains_ref, out_ref, slab_ref, both_ref, turned_a_ref, gain_ref, ghost_ref, again_ref, courant_ref, sems, *, comps
):
    padded = slab_ref.shape[0]
    rows = comps + 6
    groups = padded // rows
    total = groups * comps
    half = both_ref.shape[0] // 2
    loads = ((packed_ref, slab_ref), (stacked_ref, both_ref), (turned_ref, turned_a_ref), (gains_ref, gain_ref))
    copies = [pltpu.make_async_copy(source, target, sems.at[i]) for i, (source, target) in enumerate(loads)]
    for copy in copies:
        copy.start()
    copies[0].wait()
    lane = iota((rows - LANES, LANES), 1)
    columns = jnp.concatenate([slab_ref[(g + 1) * rows - 8:(g + 1) * rows, :] for g in range(groups)] + [jnp.zeros((LANES - 8 * groups, LANES), F32)], axis=0).T
    for g in range(groups):
        start = g * rows
        at = 8 * g + 2
        tail = columns[:, at + 3:at + 4]
        high, low, courant = (jnp.broadcast_to(tail[STEP * i:STEP * (i + 1)], (STEP, LANES)) for i in range(3))
        ghost_ref[start:start + LANES, :] = pltpu.roll(columns, LANES - at - 1, 1)
        ghost_ref[start + LANES:start + rows, :] = jnp.where(lane == 0, low, high)
        courant_ref[start:start + LANES, :] = jnp.broadcast_to(columns[:, at + 2:at + 3], (LANES, LANES))
        courant_ref[start + LANES:start + rows, :] = courant
    blocks = [slice(start, start + BLOCK) for start in range(0, padded, BLOCK)]

    def pairs_and_scale(refs):
        rounded = jnp.concatenate([ref[...].astype(BF16) for ref in refs], axis=1)
        left = jnp.dot(both_ref[0:half, :], rounded, preferred_element_type=F32)
        right = jnp.dot(both_ref[half:2 * half, :], rounded, preferred_element_type=F32)
        squares = jnp.concatenate(
            [sum(jnp.sum(jnp.square(ref[g * rows:g * rows + comps, :]), axis=0, keepdims=True) for g in range(groups)) for ref in refs], axis=1
        )
        spread = jnp.sqrt(squares / total + 1e-06)
        return (left * right).astype(BF16), 1.0 / (1.0 + DISSIPATION * spread)

    for copy in copies[1:]:
        copy.wait()
    pairs, scale = pairs_and_scale((slab_ref, ghost_ref))
    lane = iota((BLOCK, LANES), 1)
    sea = slab_ref[rows - 2:rows - 1, :]
    for block in blocks:
        gain = gain_ref[block, :]
        transfer = jnp.dot(turned_a_ref[block, :], pairs, preferred_element_type=F32)
        field, ghost = (
            (ref[block, :] + gain * ref[block, :] + transfer[:, i * LANES:(i + 1) * LANES]) * scale[:, i * LANES:(i + 1) * LANES]
            for i, ref in enumerate((slab_ref, ghost_ref))
        )
        left = jnp.where(lane == 0, ghost, pltpu.roll(field, 1, 1))
        right = jnp.where(lane == LANES - 1, ghost, pltpu.roll(field, LANES - 1, 1))
        courant = courant_ref[block, :]
        speed = jnp.abs(courant)
        again_ref[block, :] = ((1.0 - speed) * field + speed * jnp.where(courant > 0, left, right)) * sea
    pairs, scale = pairs_and_scale((again_ref,))
    copies = []
    for i, block in enumerate(blocks):
        moved = again_ref[block, :]
        transfer = jnp.dot(turned_a_ref[block, :], pairs, preferred_element_type=F32)
        courant_ref[block, :] = (moved + gain_ref[block, :] * moved + transfer) * scale
        copy = pltpu.make_async_copy(courant_ref.at[block], out_ref.at[block], sems.at[len(loads) + i])
        copy.start()
        copies.append(copy)
    for copy in copies:
        copy.wait()


def plan_body(block_ref, column_ref, offsets_ref, pick_ref, relay_ref, place_ref):
    n = column_ref.shape[0]
    rows = SLAB * n
    slots = NB_BLOCK // n
    span = NB_BLOCK // 2
    block = block_ref[0:1, 0:1]
    column = column_ref[...]

    def ones(mask):
        return mask.astype(F32).astype(BF16)

    device = iota((n, 1), 0)
    start = jnp.sum(jnp.where(device < block, column, 0), axis=0, keepdims=True)
    count = jnp.sum(jnp.where(device == block, column, 0), axis=0, keepdims=True)
    shift = lax.rem(start, jnp.int32(n))
    lane = iota((1, rows), 1)
    at = lane // SLAB
    slot = lane % SLAB
    wraps = at < shift
    base = jnp.where(wraps, at - shift + n, at - shift)
    line = lax.div(start, jnp.int32(n)) + slot + jnp.where(wraps, 1, 0)
    table = offsets_ref[...]
    wanted = jnp.sum(jnp.where(iota(table.shape, 0) == line, table, 0), axis=0, keepdims=True)
    wanted = jnp.where(jnp.logical_and(slot < slots, base + n * slot < count), wanted, -1)
    pick_ref[...] = ones(iota(pick_ref.shape, 0) == wanted)

    wide = jnp.broadcast_to(column, (n, rows))
    source = iota((n, rows), 0)
    target = iota((n, rows), 1) // SLAB
    starts = jnp.sum(jnp.where(source < target, wide, 0), axis=0, keepdims=True)
    counts = jnp.sum(jnp.where(source == target, wide, 0), axis=0, keepdims=True)
    position = lax.rem(block - starts + 128 * n, jnp.int32(n)) + n * slot
    entry = jnp.where(jnp.logical_and(position < counts, slot < slots), starts + position, -(1 << 20))
    row = iota((rows, 1), 0)
    half = row % SLAB
    place = row // SLAB
    window = jnp.where(place < n // 2, span * place + counts[:, 0:1], span * (place - n // 2)) + n * half
    size = jnp.where(half == 0, n, jnp.where(half == 1, span - n, 0))
    inside = entry - window
    relay_ref[...] = ones(jnp.logical_and(inside >= 0, inside < size))

    own = jnp.where(block < n // 2, span * block + column[0:1, 0:1], span * (block - n // 2))
    goal = lax.rem(place - own + 256 * n, jnp.int32(n)) + n * half
    place_ref[...] = ones(jnp.logical_and(iota((rows, LANES), 1) == goal, half < 2))


def gather_body(pick_ref, slab_ref, out_ref, *, slots):
    chunks = slab_ref.shape[0]
    comps = slab_ref.shape[1] - 6
    rows = pick_ref.shape[1]
    picked = jnp.zeros((comps, rows), F32)
    for k in range(chunks):
        picked = picked + exact_dot(slab_ref[k, 0:comps, :], pick_ref[k * LANES:(k + 1) * LANES, :], ((1,), (0,)))
    side = 2 * LANES
    turned = jnp.concatenate([picked, jnp.zeros((side - comps, rows), F32)], axis=0).T
    out_ref[...] = fold(turned, slots, comps - LANES)


def fold(turned, slots, rest):
    rows = turned.shape[0]
    slot = iota((rows, LANES), 0) % SLAB
    lane = iota((rows, LANES), 1)
    main = turned[:, 0:LANES]
    side = turned[:, LANES:2 * LANES]
    out = jnp.where(slot < slots, main, 0.0)
    for t in range(slots):
        part = pltpu.roll(side, slots - t, 0)
        part = part if t == 0 else pltpu.roll(part, t * rest, 1)
        inside = jnp.logical_and(lane >= t * rest, lane < (t + 1) * rest)
        out = jnp.where(jnp.logical_and(slot == slots, inside), part, out)
    return out


def unfold(value, slots, rest):
    rows = value.shape[0]
    slot = iota((rows, LANES), 0) % SLAB
    lane = iota((rows, LANES), 1)
    side = jnp.zeros((rows, LANES), F32)
    for t in range(slots):
        part = pltpu.roll(value, rows - (slots - t), 0)
        part = part if t == 0 else pltpu.roll(part, LANES - t * rest, 1)
        side = jnp.where(jnp.logical_and(slot == t, lane < rest), part, side)
    return jnp.concatenate([jnp.where(slot < slots, value, 0.0), side], axis=1)


def relay_body(chosen_ref, in_ref, out_ref, *, slots, rest):
    out_ref[...] = fold(exact_pick(chosen_ref[...], unfold(in_ref[...], slots, rest)), 2, rest)


def settle_body(chosen_ref, in_ref, out_ref):
    comps, span = out_ref.shape
    value = exact_dot(unfold(in_ref[...], 2, comps - LANES).T, chosen_ref[...], ((1,), (0,)))
    out_ref[...] = value[0:comps, 0:span]


def per_device(spectrum, courant, growth, quad_a, quad_b, sea_mask, nest_counts, nest_offsets):
    comps, points = spectrum.shape
    total = growth.shape[0]
    groups = lax.axis_size("comp")
    n = lax.axis_size("pts")
    chunks = points // LANES
    padded = 2 * LANES
    packed = jax.ShapeDtypeStruct((chunks, comps + 6, LANES), F32)
    edge = jax.ShapeDtypeStruct((8, padded), F32)
    slab = jax.ShapeDtypeStruct((SLAB * n, LANES), F32)

    zero = jnp.zeros((), F32)
    side = lax.pad(sea_mask, jnp.int32(0), ((0, points, 0),)).astype(F32) + lax.pad(courant, zero, ((points, points - comps, 0),))
    side = side.reshape(2, points)
    block = jnp.full((1, LANES), lax.axis_index("pts"), jnp.int32)
    swap, hop = call(edges_body, (edge, edge), (VMEM,) * 3, (VMEM, VMEM))(block, spectrum, side)
    both_ways = [(i, i + 1) for i in range(n - 1)]
    swap = lax.ppermute(swap, "pts", [pair for i, j in both_ways[0::2] for pair in ((i, j), (j, i))])
    hop = lax.ppermute(hop, "pts", [pair for i, j in both_ways[1::2] for pair in ((i, j), (j, i))])
    slabs = call(
        pack_body, packed, (VMEM,) * 5, HBM, scratch=(pltpu.VMEM(packed.shape, F32), pltpu.SemaphoreType.DMA((chunks,)))
    )(block, spectrum, side, swap, hop)
    slabs = lax.all_to_all(slabs, "comp", split_axis=0, concat_axis=0, tiled=True)

    column = nest_counts.reshape(n, 1)
    lines = jnp.repeat(jnp.pad(nest_offsets, (0, 4 * n)).reshape(-1, n), SLAB, axis=1)
    pick, relay, place = call(
        plan_body,
        tuple(jax.ShapeDtypeStruct(shape, BF16) for shape in ((points, SLAB * n), (SLAB * n, SLAB * n), (SLAB * n, LANES))),
        (VMEM,) * 3,
        (VMEM,) * 3,
    )(block, column, lines)
    rows = groups * (comps + 6)
    half = quad_a.shape[0]
    wide = jax.ShapeDtypeStruct((rows, LANES), F32)
    both, turned_a, gain = call(
        functools.partial(stack_body, comps=comps),
        (jax.ShapeDtypeStruct((2 * half, rows), BF16), jax.ShapeDtypeStruct((rows, half), BF16), wide),
        (VMEM,) * 3,
        (VMEM,) * 3,
        vmem=40,
    )(quad_a.T, quad_b.T, growth.reshape(1, total))
    result = call(
        functools.partial(steps_body, comps=comps),
        wide,
        (HBM, HBM, HBM, HBM),
        HBM,
        scratch=(
            pltpu.VMEM((rows, LANES), F32),
            pltpu.VMEM((2 * half, rows), BF16),
            pltpu.VMEM((rows, half), BF16),
            pltpu.VMEM((rows, LANES), F32),
            pltpu.VMEM((rows, LANES), F32),
            pltpu.VMEM((rows, LANES), F32),
            pltpu.VMEM((rows, LANES), F32),
            pltpu.SemaphoreType.DMA((4 + rows // BLOCK,)),
        ),
        vmem=58,
    )(slabs.reshape(rows, LANES), both, turned_a, gain)
    result = result.reshape(packed.shape)
    result = lax.all_to_all(result, "comp", split_axis=0, concat_axis=0, tiled=True)

    slots = NB_BLOCK // n
    sent = call(functools.partial(gather_body, slots=slots), slab, (VMEM,) * 2)(pick, result)
    sent = lax.all_to_all(sent, "pts", split_axis=0, concat_axis=0, tiled=True)
    field = result[:, 0:comps].transpose(1, 0, 2).reshape(comps, points)
    sent = call(functools.partial(relay_body, slots=slots, rest=comps - LANES), slab, (VMEM,) * 2)(relay, sent)
    sent = lax.all_to_all(sent, "pts", split_axis=0, concat_axis=0, tiled=True)
    nest = call(settle_body, jax.ShapeDtypeStruct((comps, NB_BLOCK // 2), F32), (VMEM,) * 2)(place, sent)
    return (field, nest)


def solution(mesh):
    return jax.shard_map(
        per_device,
        mesh=mesh,
        in_specs=(P("comp", "pts"), P("comp"), P(), P(), P(), P("pts"), P(), P()),
        out_specs=(P("comp", "pts"), P("comp", "pts")),
        check_vma=False,
    )
```

```python
import functools

import jax
import jax.numpy as jnp
from jax import lax
from jax.experimental import pallas as pl
from jax.experimental.pallas import tpu as pltpu
from jax.sharding import PartitionSpec as P

STEPS = 2
LANES = 128
NB_BLOCK = 192
SLAB = 4
BLOCK = 336
DISSIPATION = 0.5

F32 = jnp.float32
BF16 = jnp.bfloat16
VMEM = pl.BlockSpec(memory_space=pltpu.VMEM)
HBM = pl.BlockSpec(memory_space=pltpu.HBM)


def call(body, out_shape, ins, outs=VMEM, scratch=(), vmem=8):
    return pl.pallas_call(
        body,
        out_shape=out_shape,
        in_specs=list(ins),
        out_specs=outs,
        scratch_shapes=list(scratch),
        compiler_params=pltpu.CompilerParams(vmem_limit_bytes=vmem << 20),
        cost_estimate=pl.CostEstimate(flops=1_000_000, bytes_accessed=1_000_000, transcendentals=0),
    )


def iota(shape, axis):
    return lax.broadcasted_iota(jnp.int32, shape, axis)


def split3(value):
    high = value.astype(BF16)
    rest = value - high.astype(F32)
    middle = rest.astype(BF16)
    low = (rest - middle.astype(F32)).astype(BF16)
    return high, middle, low


def exact_dot(value, chosen, dims):
    high, middle, low = (lax.dot_general(term, chosen, (dims, ((), ())), preferred_element_type=F32) for term in split3(value))
    return (high + middle) + low


def exact_pick(chosen, value):
    high, middle, low = (lax.dot_general(chosen, term, (((1,), (0,)), ((), ())), preferred_element_type=F32) for term in split3(value))
    return (high + middle) + low


def edges_body(block_ref, field_ref, side_ref, pair_ref, next_ref):
    comps, points = field_ref.shape
    padded = pair_ref.shape[1]
    payloads = []
    for start, order in ((points - LANES, (LANES - 1, LANES - 2)), (0, (0, 1))):
        tile = jnp.concatenate([field_ref[:, start:start + LANES], jnp.zeros((padded - comps, LANES), F32)], axis=0)
        turned = tile.T
        point = start + order[0]
        sea = jnp.broadcast_to(side_ref[0:1, point:point + 1], (1, padded))
        payloads.append(jnp.concatenate([turned[lane:lane + 1, :] for lane in order] + [sea, jnp.zeros((5, padded), F32)], axis=0))
    up, down = payloads
    even = lax.rem(block_ref[0:1, 0:1], jnp.int32(2)) == 0
    pair_ref[...] = jnp.where(even, up, down)
    next_ref[...] = jnp.where(even, down, up)


STEP = 40


def rows_of(chosen, value):
    high, middle, low = (lax.dot_general(chosen, term, (((1,), (1,)), ((), ())), preferred_element_type=F32) for term in split3(value))
    return (high + middle) + low


def pack_body(block_ref, field_ref, side_ref, pair_ref, next_ref, out_ref, slab_ref, sems):
    comps, points = field_ref.shape
    chunks = points // LANES
    padded = pair_ref.shape[1]
    even = lax.rem(block_ref[0:1, 0:1], jnp.int32(2)) == 0
    before = jnp.where(even, next_ref[...], pair_ref[...])
    after = jnp.where(even, pair_ref[...], next_ref[...])
    courant_row = side_ref[1:2, 0:padded]
    columns = jnp.concatenate([before[0:1], after[0:1], courant_row, jnp.zeros((5, padded), F32)], axis=0).T[:comps, :]

    def wide(at):
        return jnp.broadcast_to(columns[:, at:at + 1], (comps, LANES))

    near_before, near_after, courant = wide(0), wide(1), wide(2)
    speed = jnp.abs(courant)
    stay = 1.0 - speed
    forward = courant > 0
    lane = iota((comps, LANES), 1)

    tiles = [field_ref[:, k * LANES:(k + 1) * LANES] for k in range(chunks)]
    ups = [pltpu.roll(tile, 1, 1) for tile in tiles]
    downs = [pltpu.roll(tile, LANES - 1, 1) for tile in tiles]
    moved = []
    copies = []
    for k in range(chunks):
        left = jnp.where(lane == 0, near_before if k == 0 else ups[k - 1], ups[k])
        right = jnp.where(lane == LANES - 1, near_after if k == chunks - 1 else downs[k + 1], downs[k])
        sea = side_ref[0:1, k * LANES:(k + 1) * LANES]
        value = (stay * tiles[k] + speed * jnp.where(forward, left, right)) * sea
        slab_ref[k, 0:comps, :] = value
        moved.append(value)

    count = 2 * chunks
    row = iota((count, LANES), 0)
    at = iota((count, LANES), 1)

    def picked(value, last_to, first_to):
        mask = jnp.logical_or(jnp.logical_and(at == LANES - 1, row == last_to), jnp.logical_and(at == 0, row == first_to))
        return rows_of(mask.astype(F32).astype(BF16), value)

    ghosts = sum(picked(moved[k], k + 1 if k < chunks - 1 else -1, chunks + k - 1 if k > 0 else -1) for k in range(chunks))
    outer = picked(tiles[0], -1, 0) + picked(tiles[chunks - 1], 1, -1)
    gap = jnp.zeros((count, padded - comps), F32)
    ghosts, outer = (jnp.concatenate([value, gap], axis=1) for value in (ghosts, outer))
    speed_row = jnp.abs(courant_row)
    stay_row = 1.0 - speed_row
    forward_row = courant_row > 0
    moved_before = (stay_row * before[0:1] + speed_row * jnp.where(forward_row, before[1:2], outer[0:1])) * before[2:3]
    moved_after = (stay_row * after[0:1] + speed_row * jnp.where(forward_row, outer[1:2], after[1:2])) * after[2:3]
    row = iota((count, padded), 0)
    ghosts = jnp.where(row == 0, moved_before, jnp.where(row == count - 1, moved_after, ghosts))
    head = ghosts[:, 0:LANES]
    tail = ghosts[:, LANES:2 * LANES]
    mixed = tail[chunks:count] + pltpu.roll(tail[0:chunks], STEP, 1) + pltpu.roll(courant_row[:, LANES:2 * LANES], 2 * STEP, 1)
    for k in range(chunks):
        slab_ref[k, comps:comps + 1, :] = head[chunks + k:chunks + k + 1]
        slab_ref[k, comps + 1:comps + 2, :] = head[k:k + 1]
        slab_ref[k, comps + 2:comps + 3, :] = courant_row[:, 0:LANES]
        slab_ref[k, comps + 3:comps + 4, :] = mixed[k:k + 1]
        slab_ref[k, comps + 4:comps + 5, :] = side_ref[0:1, k * LANES:(k + 1) * LANES]
        slab_ref[k, comps + 5:comps + 6, :] = jnp.zeros((1, LANES), F32)
        copy = pltpu.make_async_copy(slab_ref.at[k], out_ref.at[k], sems.at[k])
        copy.start()
        copies.append(copy)
    for copy in copies:
        copy.wait()


def stack_body(a_ref, b_ref, growth_ref, both_ref, turned_ref, gain_ref, *, comps):
    total, half = a_ref.shape
    rows = comps + 6
    groups = total // comps
    gap = jnp.zeros((rows - comps, half), F32)
    for at, ref in ((0, a_ref), (half, b_ref)):
        whole = ref[...].astype(F32)
        spread = jnp.concatenate([part for g in range(groups) for part in (whole[g * comps:(g + 1) * comps], gap)], axis=0)
        if at == 0:
            turned_ref[...] = spread.astype(BF16)
        for start in range(0, half, LANES):
            both_ref[at + start:at + start + LANES, :] = spread[:, start:start + LANES].T.astype(BF16)
    growth = growth_ref[...]
    column = jnp.broadcast_to(growth, (8, total)).T[:, 0:1]
    for g in range(groups):
        gain_ref[g * rows:g * rows + comps, :] = jnp.broadcast_to(column[g * comps:(g + 1) * comps], (comps, LANES))
        gain_ref[g * rows + comps:(g + 1) * rows, :] = jnp.zeros((rows - comps, LANES), F32)


def steps_body(
    packed_ref, stacked_ref, turned_ref, gains_ref, out_ref, slab_ref, both_ref, turned_a_ref, gain_ref, ghost_ref, again_ref, courant_ref, sems, *, comps
):
    padded = slab_ref.shape[0]
    rows = comps + 6
    groups = padded // rows
    total = groups * comps
    half = both_ref.shape[0] // 2
    loads = ((packed_ref, slab_ref), (stacked_ref, both_ref), (turned_ref, turned_a_ref), (gains_ref, gain_ref))
    copies = [pltpu.make_async_copy(source, target, sems.at[i]) for i, (source, target) in enumerate(loads)]
    copies[0].start()
    copies[0].wait()
    for copy in copies[1:]:
        copy.start()
    lane = iota((rows - LANES, LANES), 1)
    columns = jnp.concatenate([slab_ref[(g + 1) * rows - 8:(g + 1) * rows, :] for g in range(groups)] + [jnp.zeros((LANES - 8 * groups, LANES), F32)], axis=0).T
    for g in range(groups):
        start = g * rows
        at = 8 * g + 2
        tail = columns[:, at + 3:at + 4]
        high, low, courant = (jnp.broadcast_to(tail[STEP * i:STEP * (i + 1)], (STEP, LANES)) for i in range(3))
        ghost_ref[start:start + LANES, :] = pltpu.roll(columns, LANES - at - 1, 1)
        ghost_ref[start + LANES:start + rows, :] = jnp.where(lane == 0, low, high)
        courant_ref[start:start + LANES, :] = jnp.broadcast_to(columns[:, at + 2:at + 3], (LANES, LANES))
        courant_ref[start + LANES:start + rows, :] = courant
    blocks = [slice(start, start + BLOCK) for start in range(0, padded, BLOCK)]

    def pairs_and_scale(refs):
        rounded = jnp.concatenate([ref[...].astype(BF16) for ref in refs], axis=1)
        left = jnp.dot(both_ref[0:half, :], rounded, preferred_element_type=F32)
        right = jnp.dot(both_ref[half:2 * half, :], rounded, preferred_element_type=F32)
        squares = jnp.concatenate(
            [sum(jnp.sum(jnp.square(ref[g * rows:g * rows + comps, :]), axis=0, keepdims=True) for g in range(groups)) for ref in refs], axis=1
        )
        spread = jnp.sqrt(squares / total + 1e-06)
        return (left * right).astype(BF16), 1.0 / (1.0 + DISSIPATION * spread)

    for copy in copies[1:]:
        copy.wait()
    pairs, scale = pairs_and_scale((slab_ref, ghost_ref))
    lane = iota((BLOCK, LANES), 1)
    sea = slab_ref[rows - 2:rows - 1, :]
    for block in blocks:
        gain = gain_ref[block, :]
        transfer = jnp.dot(turned_a_ref[block, :], pairs, preferred_element_type=F32)
        field, ghost = (
            (ref[block, :] + gain * ref[block, :] + transfer[:, i * LANES:(i + 1) * LANES]) * scale[:, i * LANES:(i + 1) * LANES]
            for i, ref in enumerate((slab_ref, ghost_ref))
        )
        left = jnp.where(lane == 0, ghost, pltpu.roll(field, 1, 1))
        right = jnp.where(lane == LANES - 1, ghost, pltpu.roll(field, LANES - 1, 1))
        courant = courant_ref[block, :]
        speed = jnp.abs(courant)
        again_ref[block, :] = ((1.0 - speed) * field + speed * jnp.where(courant > 0, left, right)) * sea
    pairs, scale = pairs_and_scale((again_ref,))
    copies = []
    for i, block in enumerate(blocks):
        moved = again_ref[block, :]
        transfer = jnp.dot(turned_a_ref[block, :], pairs, preferred_element_type=F32)
        courant_ref[block, :] = (moved + gain_ref[block, :] * moved + transfer) * scale
        copy = pltpu.make_async_copy(courant_ref.at[block], out_ref.at[block], sems.at[len(loads) + i])
        copy.start()
        copies.append(copy)
    for copy in copies:
        copy.wait()


def plan_body(block_ref, column_ref, offsets_ref, pick_ref, relay_ref, place_ref):
    n = column_ref.shape[0]
    rows = SLAB * n
    slots = NB_BLOCK // n
    span = NB_BLOCK // 2
    block = block_ref[0:1, 0:1]
    column = column_ref[...]

    def ones(mask):
        return mask.astype(F32).astype(BF16)

    device = iota((n, 1), 0)
    start = jnp.sum(jnp.where(device < block, column, 0), axis=0, keepdims=True)
    count = jnp.sum(jnp.where(device == block, column, 0), axis=0, keepdims=True)
    shift = lax.rem(start, jnp.int32(n))
    lane = iota((1, rows), 1)
    at = lane // SLAB
    slot = lane % SLAB
    wraps = at < shift
    base = jnp.where(wraps, at - shift + n, at - shift)
    line = lax.div(start, jnp.int32(n)) + slot + jnp.where(wraps, 1, 0)
    table = offsets_ref[...]
    wanted = jnp.sum(jnp.where(iota(table.shape, 0) == line, table, 0), axis=0, keepdims=True)
    wanted = jnp.where(jnp.logical_and(slot < slots, base + n * slot < count), wanted, -1)
    pick_ref[...] = ones(iota(pick_ref.shape, 0) == wanted)

    wide = jnp.broadcast_to(column, (n, rows))
    source = iota((n, rows), 0)
    target = iota((n, rows), 1) // SLAB
    starts = jnp.sum(jnp.where(source < target, wide, 0), axis=0, keepdims=True)
    counts = jnp.sum(jnp.where(source == target, wide, 0), axis=0, keepdims=True)
    position = lax.rem(block - starts + 128 * n, jnp.int32(n)) + n * slot
    entry = jnp.where(jnp.logical_and(position < counts, slot < slots), starts + position, -(1 << 20))
    row = iota((rows, 1), 0)
    half = row % SLAB
    place = row // SLAB
    window = jnp.where(place < n // 2, span * place + counts[:, 0:1], span * (place - n // 2)) + n * half
    size = jnp.where(half == 0, n, jnp.where(half == 1, span - n, 0))
    inside = entry - window
    relay_ref[...] = ones(jnp.logical_and(inside >= 0, inside < size))

    own = jnp.where(block < n // 2, span * block + column[0:1, 0:1], span * (block - n // 2))
    goal = lax.rem(place - own + 256 * n, jnp.int32(n)) + n * half
    place_ref[...] = ones(jnp.logical_and(iota((rows, LANES), 1) == goal, half < 2))


def gather_body(pick_ref, slab_ref, out_ref, *, slots):
    chunks = slab_ref.shape[0]
    comps = slab_ref.shape[1] - 6
    rows = pick_ref.shape[1]
    picked = jnp.zeros((comps, rows), F32)
    for k in range(chunks):
        picked = picked + exact_dot(slab_ref[k, 0:comps, :], pick_ref[k * LANES:(k + 1) * LANES, :], ((1,), (0,)))
    side = 2 * LANES
    turned = jnp.concatenate([picked, jnp.zeros((side - comps, rows), F32)], axis=0).T
    out_ref[...] = fold(turned, slots, comps - LANES)


def fold(turned, slots, rest):
    rows = turned.shape[0]
    slot = iota((rows, LANES), 0) % SLAB
    lane = iota((rows, LANES), 1)
    main = turned[:, 0:LANES]
    side = turned[:, LANES:2 * LANES]
    out = jnp.where(slot < slots, main, 0.0)
    for t in range(slots):
        part = pltpu.roll(side, slots - t, 0)
        part = part if t == 0 else pltpu.roll(part, t * rest, 1)
        inside = jnp.logical_and(lane >= t * rest, lane < (t + 1) * rest)
        out = jnp.where(jnp.logical_and(slot == slots, inside), part, out)
    return out


def unfold(value, slots, rest):
    rows = value.shape[0]
    slot = iota((rows, LANES), 0) % SLAB
    lane = iota((rows, LANES), 1)
    side = jnp.zeros((rows, LANES), F32)
    for t in range(slots):
        part = pltpu.roll(value, rows - (slots - t), 0)
        part = part if t == 0 else pltpu.roll(part, LANES - t * rest, 1)
        side = jnp.where(jnp.logical_and(slot == t, lane < rest), part, side)
    return jnp.concatenate([jnp.where(slot < slots, value, 0.0), side], axis=1)


def relay_body(chosen_ref, in_ref, out_ref, *, slots, rest):
    out_ref[...] = fold(exact_pick(chosen_ref[...], unfold(in_ref[...], slots, rest)), 2, rest)


def settle_body(chosen_ref, in_ref, out_ref):
    comps, span = out_ref.shape
    value = exact_dot(unfold(in_ref[...], 2, comps - LANES).T, chosen_ref[...], ((1,), (0,)))
    out_ref[...] = value[0:comps, 0:span]


def per_device(spectrum, courant, growth, quad_a, quad_b, sea_mask, nest_counts, nest_offsets):
    comps, points = spectrum.shape
    total = growth.shape[0]
    groups = lax.axis_size("comp")
    n = lax.axis_size("pts")
    chunks = points // LANES
    padded = 2 * LANES
    packed = jax.ShapeDtypeStruct((chunks, comps + 6, LANES), F32)
    edge = jax.ShapeDtypeStruct((8, padded), F32)
    slab = jax.ShapeDtypeStruct((SLAB * n, LANES), F32)

    zero = jnp.zeros((), F32)
    side = lax.pad(sea_mask, jnp.int32(0), ((0, points, 0),)).astype(F32) + lax.pad(courant, zero, ((points, points - comps, 0),))
    side = side.reshape(2, points)
    block = jnp.full((1, LANES), lax.axis_index("pts"), jnp.int32)
    swap, hop = call(edges_body, (edge, edge), (VMEM,) * 3, (VMEM, VMEM))(block, spectrum, side)
    both_ways = [(i, i + 1) for i in range(n - 1)]
    swap = lax.ppermute(swap, "pts", [pair for i, j in both_ways[0::2] for pair in ((i, j), (j, i))])
    hop = lax.ppermute(hop, "pts", [pair for i, j in both_ways[1::2] for pair in ((i, j), (j, i))])
    slabs = call(
        pack_body, packed, (VMEM,) * 5, HBM, scratch=(pltpu.VMEM(packed.shape, F32), pltpu.SemaphoreType.DMA((chunks,)))
    )(block, spectrum, side, swap, hop)
    slabs = lax.all_to_all(slabs, "comp", split_axis=0, concat_axis=0, tiled=True)

    column = nest_counts.reshape(n, 1)
    lines = jnp.repeat(jnp.pad(nest_offsets, (0, 4 * n)).reshape(-1, n), SLAB, axis=1)
    pick, relay, place = call(
        plan_body,
        tuple(jax.ShapeDtypeStruct(shape, BF16) for shape in ((points, SLAB * n), (SLAB * n, SLAB * n), (SLAB * n, LANES))),
        (VMEM,) * 3,
        (VMEM,) * 3,
    )(block, column, lines)
    rows = groups * (comps + 6)
    half = quad_a.shape[0]
    wide = jax.ShapeDtypeStruct((rows, LANES), F32)
    both, turned_a, gain = call(
        functools.partial(stack_body, comps=comps),
        (jax.ShapeDtypeStruct((2 * half, rows), BF16), jax.ShapeDtypeStruct((rows, half), BF16), wide),
        (VMEM,) * 3,
        (VMEM,) * 3,
        vmem=40,
    )(quad_a.T, quad_b.T, growth.reshape(1, total))
    result = call(
        functools.partial(steps_body, comps=comps),
        wide,
        (HBM, HBM, HBM, HBM),
        HBM,
        scratch=(
            pltpu.VMEM((rows, LANES), F32),
            pltpu.VMEM((2 * half, rows), BF16),
            pltpu.VMEM((rows, half), BF16),
            pltpu.VMEM((rows, LANES), F32),
            pltpu.VMEM((rows, LANES), F32),
            pltpu.VMEM((rows, LANES), F32),
            pltpu.VMEM((rows, LANES), F32),
            pltpu.SemaphoreType.DMA((4 + rows // BLOCK,)),
        ),
        vmem=58,
    )(slabs.reshape(rows, LANES), both, turned_a, gain)
    result = result.reshape(packed.shape)
    result = lax.all_to_all(result, "comp", split_axis=0, concat_axis=0, tiled=True)

    slots = NB_BLOCK // n
    sent = call(functools.partial(gather_body, slots=slots), slab, (VMEM,) * 2)(pick, result)
    sent = lax.all_to_all(sent, "pts", split_axis=0, concat_axis=0, tiled=True)
    field = result[:, 0:comps].transpose(1, 0, 2).reshape(comps, points)
    sent = call(functools.partial(relay_body, slots=slots, rest=comps - LANES), slab, (VMEM,) * 2)(relay, sent)
    sent = lax.all_to_all(sent, "pts", split_axis=0, concat_axis=0, tiled=True)
    nest = call(settle_body, jax.ShapeDtypeStruct((comps, NB_BLOCK // 2), F32), (VMEM,) * 2)(place, sent)
    return (field, nest)


def solution(mesh):
    return jax.shard_map(
        per_device,
        mesh=mesh,
        in_specs=(P("comp", "pts"), P("comp"), P(), P(), P(), P("pts"), P(), P()),
        out_specs=(P("comp", "pts"), P("comp", "pts")),
        check_vma=False,
    )
```
